32 devices in a mesh: slab: 4 (over y, x), rcv: 8 (over z, core).
Axes of the slice: x: 2, y: 2, z: 4, core: 2. Of those that a mesh axis runs over, the one named last changes fastest.
Arguments:
- adjoint_now: float32 [8, 16, 128, 128], P('rcv', 'slab'), may hold values from -6 to 6
- adjoint_before: float32 [8, 16, 128, 128], P('rcv', 'slab'), may hold values from -6 to 6
- courant_field: float32 [16, 128, 128], P('slab'), may hold values from 0.04 to 0.2
- log_buoyancy: float32 [16, 128, 128], P('slab'), may hold values from -0.3 to 0.3
- snapshot_store: float32 [8, 16, 128, 128], P('rcv', 'slab'), may hold values from -6 to 6
- owner_order: int32 [8], replicated, may hold values from 0 to 7, each once
- receiver_cells: int32 [8], P('rcv'), may hold values from 0 to 262143
- receiver_traces: float32 [8, 8], P('rcv'), may hold values from -6 to 6
- residual_weights: float32 [8], P('rcv'), may hold values from -0.3 to 0.3
Outputs:
- sensitivity: float32 [16, 128, 128], P('slab', 'rcv')
- adjoint_after: float32 [8, 16, 128, 128], P('rcv', 'slab')
The draws below stay inside these ranges and needn't reach their ends.
Inputs may be any that keep to these rules, and one draw needn't show every extreme that they name: Each slot number appears once; checkpoint k reads slot owner_order[k] for k < 4. `receiver_cells`: a cell of the grid.
All inputs are finite; a program needn't handle non-finite values.
Results may differ from the reference program's by a relative error of at most 0.0003.
Values sent between devices are 32-bit elements; how exact they have to be, the bound alone decides.
No kernel may reach another device: no remote copies, remote signals or barrier semaphores. Data moves between devices by JAX's collectives and lax.ppermute only.
A program may use at most 64 MiB of HBM per device.

```python
import math
import jax
import jax.numpy as jnp
from jax import lax

NY = 128
NZ = 128
SNAPS = 4
NX = 16
RCVS = 8
SLOTS = 8
STEPS = 8


def place_ends(entries, key, smallest, largest):
    longest = entries.shape.index(max(entries.shape))
    spots = []
    for shift in (0, 1):
        where = [jax.random.randint(jax.random.fold_in(key, axis), (), 0, length) for axis, length in enumerate(entries.shape)]
        where[longest] = (where[longest] + shift) % entries.shape[longest]
        spots.append(tuple(where))
    return entries.at[spots[0]].set(smallest).at[spots[1]].set(largest)


def block_levels(own_key, shape, cuts, smallest, largest):
    def one(position, shards_of):
        heights = jax.random.uniform(jax.random.fold_in(jax.random.fold_in(own_key, 6), position), (shards_of,), jnp.float32, smallest / len(cuts), largest / len(cuts))
        return jnp.repeat(jnp.exp(heights), shape[position] // shards_of).reshape((-1,) + (1,) * (len(shape) - position - 1))

    gain = one(*cuts[0])
    for cut in cuts[1:]:
        gain = gain * one(*cut)
    return gain


def normal_values(stream_key, dims, scale, most, cuts=(), held_as=jnp.bfloat16):
    entries = scale * jax.random.normal(stream_key, dims, jnp.float32)
    if cuts:
        entries = entries * block_levels(stream_key, dims, cuts, -0.22, 0.18)
    return jnp.clip(entries, -most, most).astype(held_as)


def setup_inputs(seed: int = 0) -> dict:
    key_list = jax.random.split(jax.random.key(seed), 10)
    adjoint_now = normal_values(key_list[0], (RCVS, NX, NY, NZ), 1.0, 6.0, ((0, 8), (1, 4)), jnp.float32)
    adjoint_before = normal_values(key_list[1], (RCVS, NX, NY, NZ), 1.0, 6.0, ((0, 8), (1, 4)), jnp.float32)
    courant_field = jnp.clip(jnp.exp(math.log(0.2) - 1.609438 * jax.random.uniform(key_list[2], (NX, NY, NZ), jnp.float32) ** block_levels(key_list[2], (NX, NY, NZ), ((0, 4),), -0.2, 0.2)), 0.04, 0.2)
    log_buoyancy = jnp.clip(jax.random.uniform(key_list[3], (NX, NY, NZ), jnp.float32, -0.3, 0.3) * block_levels(key_list[3], (NX, NY, NZ), ((0, 4),), -0.4, 0.0), -0.3, 0.3)
    snapshot_store = normal_values(key_list[4], (SLOTS, NX, NY, NZ), 1.0, 6.0, ((0, 8), (1, 4)), jnp.float32)
    owner_order = jax.random.permutation(key_list[5], SLOTS).astype(jnp.int32)
    receiver_cells = place_ends(jax.random.randint(key_list[6], (RCVS,), 0, NX * NY * NZ), jax.random.fold_in(key_list[6], 1), 0, (NX * NY * NZ) - 1).astype(jnp.int32)
    receiver_traces = normal_values(key_list[7], (RCVS, STEPS), 1.0, 6.0, ((0, 8),), jnp.float32)
    residual_weights = normal_values(key_list[8], (RCVS,), 0.05, 0.3, ((0, 8),), jnp.float32)
    return dict(adjoint_now=adjoint_now, adjoint_before=adjoint_before, courant_field=courant_field, log_buoyancy=log_buoyancy, snapshot_store=snapshot_store, owner_order=owner_order, receiver_cells=receiver_cells, receiver_traces=receiver_traces, residual_weights=residual_weights)


def piece_of(field, axis_no, begin, extent):
    return lax.slice_in_dim(field, begin, begin + extent, axis=axis_no)


def pad_axis(field, axis_no):
    widths = [(0, 0)] * field.ndim
    widths[axis_no] = (2, 2)
    return jnp.pad(field, widths)


def second_diff(field, axis_no, extent):
    outer = piece_of(field, axis_no, 0, extent) + piece_of(field, axis_no, 4, extent)
    inner = piece_of(field, axis_no, 1, extent) + piece_of(field, axis_no, 3, extent)
    return (16.0 * inner - outer - 30.0 * piece_of(field, axis_no, 2, extent)) / 12.0


def first_diff(field, axis_no, extent):
    inner = piece_of(field, axis_no, 3, extent) - piece_of(field, axis_no, 1, extent)
    outer = piece_of(field, axis_no, 4, extent) - piece_of(field, axis_no, 0, extent)
    return (8.0 * inner - outer) / 12.0


def slopes(log_ext):
    width = log_ext.shape[0] - 4
    centre = piece_of(log_ext, 0, 2, width)
    wide_y = pad_axis(centre, 1)
    wide_z = pad_axis(centre, 2)
    return jnp.stack([first_diff(log_ext, 0, width), first_diff(wide_y, 1, centre.shape[1]), first_diff(wide_z, 2, centre.shape[2])])


def advance(field, before, courant, gradient):
    first_axis = field.ndim - 3
    width = field.shape[first_axis] - 4
    centre = piece_of(field, first_axis, 2, width)
    wide_y = pad_axis(centre, first_axis + 1)
    wide_z = pad_axis(centre, first_axis + 2)
    size_y = field.shape[first_axis + 1]
    size_z = field.shape[first_axis + 2]
    curvature = second_diff(field, first_axis, width) + second_diff(wide_y, first_axis + 1, size_y) + second_diff(wide_z, first_axis + 2, size_z)
    drift_term = gradient[0] * first_diff(field, first_axis, width) + gradient[1] * first_diff(wide_y, first_axis + 1, size_y) + gradient[2] * first_diff(wide_z, first_axis + 2, size_z)
    return 2.0 * centre - before + courant * (curvature + drift_term)


def reference(adjoint_now, adjoint_before, courant_field, log_buoyancy, snapshot_store, owner_order, receiver_cells, receiver_traces, residual_weights):
    gradient = slopes(pad_axis(log_buoyancy, 0))
    snapshots = jnp.take(snapshot_store, owner_order[:SNAPS], axis=0)
    flat_ids = jnp.arange(NX * NY * NZ, dtype=jnp.int32).reshape(NX, NY, NZ)

    def receiver(kernel, item):
        current, previous, trace_row, cell_id, weight = item
        struck = flat_ids == cell_id
        for snap_index in range(SNAPS):
            for half_step in range(2):
                tick = 2 * snap_index + half_step
                upcoming = advance(pad_axis(current, 0), previous, courant_field, gradient)
                upcoming = upcoming + jnp.where(struck, trace_row[tick], 0.0)
                previous, current = current, upcoming
            kernel = kernel + (weight * current) * snapshots[snap_index]
        return kernel, current

    start_kernel = jnp.zeros((NX, NY, NZ), jnp.float32)
    sensitivity, adjoint_after = lax.scan(receiver, start_kernel, (adjoint_now, adjoint_before, receiver_traces, receiver_cells, residual_weights))
    return sensitivity, adjoint_after
```

```python
import functools

import jax
import jax.numpy as jnp
from jax import lax
from jax.experimental import pallas as pl
from jax.experimental.pallas import tpu as pltpu
from jax.sharding import PartitionSpec as P

SNAPS = 4
PAD = 8
CHUNK = 32


VMEM = pl.BlockSpec(memory_space=pltpu.VMEM)
SMEM = pl.BlockSpec(memory_space=pltpu.SMEM)


def swap(block, axis, mask):
    peers = lax.axis_size(axis)
    return lax.ppermute(block, axis, [(i, i ^ mask) for i in range(peers)])


def call(body, outs, inputs, scalars, scratch, name, flops=0):
    size = sum(x.size * 4 for x in inputs) + sum(4 * functools.reduce(lambda a, b: a * b, o) for o in outs)
    return pl.pallas_call(
        body,
        out_shape=[jax.ShapeDtypeStruct(o, jnp.float32) for o in outs],
        in_specs=[SMEM] * len(scalars) + [VMEM] * len(inputs),
        out_specs=[VMEM] * len(outs),
        scratch_shapes=[pltpu.VMEM(s, jnp.float32) for s in scratch],
        cost_estimate=pl.CostEstimate(flops=flops, bytes_accessed=size, transcendentals=0),
        name=name,
    )(*scalars, *inputs)


def lane_shift(field, shift, lane):
    size = field.shape[-1]
    rolled = pltpu.roll(field, (-shift) % size, 1)
    inside = lane < size - shift if shift > 0 else lane >= -shift
    return jnp.where(inside, rolled, 0.0)


def neighbours(ref, x, row, count, lane):
    rows = slice(row, row + count)
    mid = ref[x, rows, :]
    along_x = [ref[x + k, rows, :] for k in (1, -1, 2, -2)]
    along_y = [ref[x, row + k : row + k + count, :] for k in (1, -1, 2, -2)]
    along_z = [lane_shift(mid, k, lane) for k in (1, -1, 2, -2)]
    return mid, (along_x, along_y, along_z)


def prepare(c_ref, b_ref, coef, planes, rows):
    size_z = b_ref.shape[2]

    def plane(x, carry):
        for start in range(0, rows, CHUNK):
            count = min(CHUNK, rows - start)
            row = PAD + start
            lane = lax.broadcasted_iota(jnp.int32, (count, size_z), 1)
            _, sides = neighbours(b_ref, x + 2, row, count, lane)
            c = c_ref[x + 2, row : row + count, :]
            coef[0, x, start : start + count, :] = 2.0 - 7.5 * c
            coef[1, x, start : start + count, :] = (4.0 / 3.0) * c
            scaled = c * (2.0 / 3.0)
            for d, (p1, m1, p2, m2) in enumerate(sides):
                slope = (8.0 * (p1 - m1) - (p2 - m2)) * (1.0 / 12.0)
                coef[2 + d, x, start : start + count, :] = scaled * slope
        return carry

    lax.fori_loop(0, planes, plane, 0)


def advance(cur, old, coef, row_lo, row_hi, x_lo, x_hi):
    size_z = cur.shape[2]

    def plane(x, carry):
        for start in range(row_lo, row_hi, CHUNK):
            count = min(CHUNK, row_hi - start)
            row = PAD + start
            lane = lax.broadcasted_iota(jnp.int32, (count, size_z), 1)
            mid, sides = neighbours(cur, x + 2, row, count, lane)
            near = far = drift = None
            for d, (p1, m1, p2, m2) in enumerate(sides):
                one, two = p1 + m1, p2 + m2
                part = coef[2 + d, x, start : start + count, :] * ((p1 - m1) - 0.125 * (p2 - m2))
                near = one if near is None else near + one
                far = two if far is None else far + two
                drift = part if drift is None else drift + part
            result = coef[0, x, start : start + count, :] * mid - old[x + 2, row : row + count, :]
            result = result + coef[1, x, start : start + count, :] * (near - 0.0625 * far) + drift
            old[x + 2, row : row + count, :] = result
        return carry

    lax.fori_loop(x_lo, x_hi, plane, 0)


def inject(ref, cell, amplitude, first_row, rows, size_y):
    size_z = ref.shape[2]
    x = cell // (size_y * size_z)
    row = (cell // size_z) % size_y - first_row
    z = cell % size_z

    @pl.when((row >= 0) & (row < rows))
    def _():
        base = pl.multiple_of((row // 8) * 8, 8)
        lane = lax.broadcasted_iota(jnp.int32, (8, size_z), 1)
        sub = lax.broadcasted_iota(jnp.int32, (8, size_z), 0)
        hit = (lane == z) & (sub == row - base)
        where = (x + 2, pl.ds(PAD + base, 8), slice(None))
        ref[where] = ref[where] + jnp.where(hit, amplitude, 0.0)


def clear_edges(refs):
    for ref in refs:
        planes = ref.shape[0]
        for x in (0, 1, planes - 2, planes - 1):
            ref[x, :, :] = jnp.zeros(ref.shape[1:], jnp.float32)


def span(step, steps, rows):
    low, high = 2 * (step + 1), rows - 2 * (step + 1)
    return low // 8 * 8, min(rows, -(-high // 8) * 8)


def pack_body(dims, ids, now, old, courant, logb, *refs):
    slabs, planes, size_y, size_z, share, halo = dims
    outs, wide = refs[:-1], refs[-1]
    window = share + 2 * halo
    half = planes // 2
    slab, core = ids[0], ids[1]
    wide[:, :, 0:halo, :] = jnp.zeros((4, planes, halo, size_z), jnp.float32)
    wide[:, :, halo + size_y :, :] = jnp.zeros((4, planes, halo, size_z), jnp.float32)
    for i, ref in enumerate((courant, logb, now, old)):
        wide[i, :, halo : halo + size_y, :] = ref[...]
    for d in range(slabs):
        first = pl.multiple_of((slab ^ d) * share, 8)
        model, state = outs[2 * d], outs[2 * d + 1]
        for i in range(2):
            if d == 0:
                model[i * planes : (i + 1) * planes] = wide[i, :, pl.ds(first, window), :]
            else:
                model[i * half : (i + 1) * half] = wide[i, pl.ds(half * core, half), pl.ds(first, window), :]
            state[i * planes : (i + 1) * planes] = wide[2 + i, :, pl.ds(first, window), :]


def field_body(dims, ids, cells, traces, *refs):
    slabs, planes, size_y, size_z, share, halo, steps = dims
    window = share + 2 * halo
    half = planes // 2
    total = planes * slabs
    models, states, others = refs[:slabs], refs[slabs : 2 * slabs], refs[2 * slabs : 3 * slabs - 1]
    outs = refs[3 * slabs - 1 : 4 * slabs - 1]
    now, old, c_ref, b_ref, coef = refs[4 * slabs - 1 :]
    slab, core = ids[0], ids[1]
    clear_edges((now, old, b_ref))
    inner = slice(PAD, PAD + window)
    for d in range(slabs):
        base = (slab ^ d) * planes + 2
        now[pl.ds(base, planes), inner, :] = states[d][:planes]
        old[pl.ds(base, planes), inner, :] = states[d][planes:]
        for i, ref in enumerate((c_ref, b_ref)):
            if d == 0:
                ref[pl.ds(base, planes), inner, :] = models[0][i * planes : (i + 1) * planes]
            else:
                ref[pl.ds(base + half * core, half), inner, :] = models[d][i * half : (i + 1) * half]
                ref[pl.ds(base + half * (1 - core), half), inner, :] = others[d - 1][i * half : (i + 1) * half]
    prepare(c_ref, b_ref, coef, total, window)
    first = slab * share - halo
    for step in range(steps):
        low, high = span(step, steps, window)
        advance(now, old, coef, low, high, 0, total)
        inject(old, cells[0], traces[0, step], first, window, size_y)
        now, old = old, now
    for d in range(slabs):
        outs[d][...] = now[pl.ds((slab ^ d) * planes + 2, planes), PAD + halo : PAD + halo + share, :]


def sum_body(dims, ids, order, cells, traces, *refs):
    slabs, planes, size_y, size_z, tile, halo, steps, groups = dims
    share = 2 * tile
    window = share + 2 * halo
    half = planes // 2
    total = planes * slabs
    mine, others, snaps = refs[:slabs], refs[slabs : 2 * slabs], refs[2 * slabs]
    out = refs[2 * slabs + 1]
    now, old, c_ref, b_ref, coef = refs[2 * slabs + 2 :]
    slab, core, chip = ids[0], ids[1], ids[2]
    clear_edges((now, old, b_ref))
    inner = slice(PAD, PAD + window)
    for d in range(slabs):
        base = (slab ^ d) * planes + 2
        for i, ref in enumerate((now, old, c_ref, b_ref)):
            ref[pl.ds(base + half * core, half), inner, :] = mine[d][i * half : (i + 1) * half]
            ref[pl.ds(base + half * (1 - core), half), inner, :] = others[d][i * half : (i + 1) * half]
    prepare(c_ref, b_ref, coef, total, window)
    first = chip * share - halo
    acc = jnp.zeros((planes, tile, size_z), jnp.float32)
    for step in range(steps):
        low, high = span(step, steps, window)
        reach = 2 * (steps - 1 - step)
        x_lo = jnp.maximum(slab * planes - reach, 0)
        x_hi = jnp.minimum((slab + 1) * planes + reach, total)
        advance(now, old, coef, low, high, x_lo, x_hi)

        def add(r, carry, target=old, step=step):
            inject(target, cells[r], traces[r, step], first, window, size_y)
            return carry

        lax.fori_loop(0, 2 * groups, add, 0)
        now, old = old, now
        if step % 2 == 1:
            slot = order[step // 2]
            piece = ((slot // 2) ^ chip) * 2 + ((slot % 2) ^ core)
            own = pl.ds(slab * planes + 2, planes)
            top = PAD + halo
            tiles = [now[own, top + i * tile : top + (i + 1) * tile, :] for i in range(2)]
            acc = acc + jnp.where(core == 0, tiles[0], tiles[1]) * snaps[piece]
    out[...] = acc


def unpack_body(dims, ids, *refs):
    slabs, share = dims
    out = refs[slabs]
    for d in range(slabs):
        out[:, pl.ds(pl.multiple_of((ids[0] ^ d) * share, 8), share), :] = refs[d][...]


def local(
    adjoint_now,
    adjoint_before,
    courant_field,
    log_buoyancy,
    snapshot_store,
    owner_order,
    receiver_cells,
    receiver_traces,
    residual_weights,
):
    planes, size_y, size_z = courant_field.shape
    steps = receiver_traces.shape[1]
    slabs, ranks = lax.axis_size("slab"), lax.axis_size("rcv")
    chips = ranks // 2
    halo = 2 * steps
    share = size_y // slabs
    tile = size_y // ranks
    half = planes // 2
    window = share + 2 * halo
    wide = 2 * tile + 2 * halo
    total = planes * slabs
    slab = lax.axis_index("slab")
    rank = lax.axis_index("rcv")
    core, chip = rank % 2, rank // 2
    ids = jnp.stack([slab, core, chip]).astype(jnp.int32)
    now, old, store = adjoint_now[0], adjoint_before[0], snapshot_store[0]

    shapes = []
    for d in range(slabs):
        shapes += [((2 * planes if d == 0 else 2 * half), window, size_z), (2 * planes, window, size_z)]
    packed = call(
        functools.partial(pack_body, (slabs, planes, size_y, size_z, share, halo)),
        shapes,
        [now, old, courant_field, log_buoyancy],
        [ids],
        [(4, planes, size_y + 2 * halo, size_z)],
        "pack",
    )
    models = [packed[0]] + [swap(packed[2 * d], "slab", d) for d in range(1, slabs)]
    states = [packed[1]] + [swap(packed[2 * d + 1], "slab", d) for d in range(1, slabs)]
    others = [swap(models[d], "rcv", 1) for d in range(1, slabs)]

    fields = residual_weights[0] * jnp.stack([now, old])
    fields = fields.reshape(2, 2, half, size_y, size_z)
    pick = functools.partial(lax.dynamic_index_in_dim, keepdims=False)
    tiles = store.reshape(planes, chips, 2, tile, size_z)
    row = jnp.concatenate([receiver_cells.astype(jnp.float32), residual_weights[0] * receiver_traces[0]])
    row = jnp.pad(row, (0, size_z - row.shape[0]))
    info = jnp.where(lax.broadcasted_iota(jnp.int32, (8, 1), 0) == core, row[None], 0.0)
    flat = lambda a: a.reshape(-1, size_z)
    sent = jnp.concatenate([flat(pick(fields, 1 - core, 1)), flat(pick(tiles, 1 - core, 2)), info])
    got = swap(sent, "rcv", 1)
    cut = 2 * half * size_y
    pair = pick(fields, core, 1) + got[:cut].reshape(2, half, size_y, size_z)
    pair = jnp.pad(pair, ((0, 0), (0, 0), (halo, halo), (0, 0)))
    tiles = jnp.stack([pick(tiles, core, 2), got[cut:-8].reshape(planes, chips, tile, size_z)])
    info = info + got[-8:]
    received = []
    for d in range(chips):
        to = chip ^ d
        rows = lax.dynamic_slice_in_dim(pair, to * 2 * tile, wide, 2)
        block = jnp.concatenate([flat(rows), flat(pick(tiles, to, 2)), info])
        received.append(swap(block, "rcv", 2 * d) if d else block)
    cut = 2 * half * wide
    summed = functools.reduce(jnp.add, [b[:cut] for b in received]).reshape(2 * half, wide, size_z)
    snaps = jnp.stack([b[cut:-8].reshape(2, planes, tile, size_z) for b in received])
    snaps = snaps.reshape(2 * chips, planes, tile, size_z)
    infos = jnp.concatenate([b[-8:-6] for b in received])
    all_cells = infos[:, 0].astype(jnp.int32)
    all_traces = infos[:, 1 : 1 + steps]

    model = jnp.stack([courant_field, log_buoyancy])
    model = lax.dynamic_slice_in_dim(model, half * core, half, 1)
    model = jnp.pad(model, ((0, 0), (0, 0), (halo, halo), (0, 0)))
    model = lax.dynamic_slice_in_dim(model, chip * 2 * tile, wide, 2)
    block = jnp.concatenate([summed, model.reshape(2 * half, wide, size_z)])
    mine = [block] + [swap(block, "slab", d) for d in range(1, slabs)]
    theirs = [swap(b, "rcv", 1) for b in mine]

    scratch = lambda rows: [(total + 4, rows + 2 * PAD, size_z)] * 4 + [(5, total, rows, size_z)]
    finals = call(
        functools.partial(field_body, (slabs, planes, size_y, size_z, share, halo, steps)),
        [(planes, share, size_z)] * slabs,
        models + states + others,
        [ids, receiver_cells, receiver_traces],
        scratch(window),
        "field",
        flops=40 * steps * total * window * size_z,
    )
    back = [finals[0]] + [swap(finals[d], "slab", d) for d in range(1, slabs)]
    (sensitivity,) = call(
        functools.partial(sum_body, (slabs, planes, size_y, size_z, tile, halo, steps, chips)),
        [(planes, tile, size_z)],
        mine + theirs + [snaps],
        [ids, owner_order, all_cells, all_traces],
        scratch(wide),
        "summed",
        flops=40 * steps * total * wide * size_z,
    )
    (after,) = call(
        functools.partial(unpack_body, (slabs, share)),
        [(planes, size_y, size_z)],
        back,
        [ids],
        [],
        "unpack",
    )
    return (sensitivity, after[None])


def solution(mesh):
    placed = (
        P("rcv", "slab", None, None),
        P("rcv", "slab", None, None),
        P("slab", None, None),
        P("slab", None, None),
        P("rcv", "slab", None, None),
        P(),
        P("rcv"),
        P("rcv", None),
        P("rcv"),
    )
    return jax.shard_map(
        local,
        mesh=mesh,
        in_specs=placed,
        out_specs=(P("slab", "rcv", None), P("rcv", "slab", None, None)),
        check_vma=False,
    )
```

```python
import functools

import jax
import jax.numpy as jnp
from jax import lax
from jax.experimental import pallas as pl
from jax.experimental.pallas import tpu as pltpu
from jax.sharding import PartitionSpec as P

SNAPS = 4
REACH = (1, -1, 2, -2)
GROUP = 8


VMEM = pl.BlockSpec(memory_space=pltpu.VMEM)
SMEM = pl.BlockSpec(memory_space=pltpu.SMEM)


def swap(block, axis, mask):
    peers = lax.axis_size(axis)
    return lax.ppermute(block, axis, [(i, i ^ mask) for i in range(peers)])


def call(body, outs, inputs, scalars, scratch, name, flops=0):
    size = sum(x.size * 4 for x in inputs) + sum(4 * functools.reduce(lambda a, b: a * b, o) for o in outs)
    return pl.pallas_call(
        body,
        out_shape=[jax.ShapeDtypeStruct(o, jnp.float32) for o in outs],
        in_specs=[SMEM] * len(scalars) + [VMEM] * len(inputs),
        out_specs=[VMEM] * len(outs),
        scratch_shapes=scratch,
        cost_estimate=pl.CostEstimate(flops=flops, bytes_accessed=size, transcendentals=0),
        name=name,
    )(*scalars, *inputs)


def band(gap, near, far, centre):
    apart = jnp.abs(gap)
    weight = jnp.where(apart == 1, near, jnp.where(apart == 2, far, 0.0))
    if centre is None:
        return jnp.where(gap < 0, -weight, weight)
    return jnp.where(apart == 0, centre, weight)


def fill_bands(lanes, rows):
    size = lanes.shape[0] // 2
    gap = lax.broadcasted_iota(jnp.int32, lanes.shape, 0) % size - lax.broadcasted_iota(jnp.int32, lanes.shape, 1) % size
    column = lax.broadcasted_iota(jnp.int32, lanes.shape, 1)
    lanes[...] = jnp.where(column < size, band(gap, 16.0, -1.0, -90.0), band(gap, 8.0, -1.0, None)).astype(jnp.bfloat16)
    size = rows.shape[0] // 2
    gap = lax.broadcasted_iota(jnp.int32, rows.shape, 1) % size - lax.broadcasted_iota(jnp.int32, rows.shape, 0) % size
    row = lax.broadcasted_iota(jnp.int32, rows.shape, 0)
    rows[...] = jnp.where(row < size, band(gap, 16.0, -1.0, 0.0), band(gap, 8.0, -1.0, None)).astype(jnp.bfloat16)


def differences(ref, x, group, bands):
    lanes, rows = bands
    count, size_z = ref.shape[1:]
    parts = []
    for j in range(group):
        field = ref[x + j]
        high = field.astype(jnp.bfloat16)
        low = (field - high.astype(jnp.float32)).astype(jnp.bfloat16)
        parts.append((high, low))
    flat = jnp.concatenate([jnp.concatenate(p, axis=1) for p in parts], axis=0)
    along_z = jnp.dot(flat, lanes[...], preferred_element_type=jnp.float32)
    along_y = []
    for j in range(0, group, 2):
        pair = jnp.concatenate([jnp.concatenate(p, axis=0) for p in parts[j : j + 2]], axis=1)
        both = jnp.dot(rows[...], pair, preferred_element_type=jnp.float32)
        along_y += [both[:, i * size_z : (i + 1) * size_z] for i in range(2)]
    return along_z, along_y


def prepare(c_ref, b_ref, coef, bands, planes):
    count, size_z = b_ref.shape[1:]
    group = min(GROUP, planes)

    def some(g, carry):
        x = g * group
        along_z, along_y = differences(b_ref, x + 2, group, bands)
        for start in range(0, count, 8):
            rows = slice(start, start + 8)
            stack = [b_ref[x + k, rows, :] for k in range(group + 4)]
            for j in range(group):
                c = c_ref[x + j + 2, rows, :]
                scaled = (1.0 / 144.0) * c
                twelfth = (1.0 / 12.0) * c
                near = 16.0 * twelfth
                p1, m1, p2, m2 = [stack[j + 2 + k] for k in REACH]
                slope = scaled * (8.0 * (p1 - m1) - (p2 - m2))
                steep = 8.0 * slope
                weights = [near + steep, near - steep, -twelfth - slope, slope - twelfth, twelfth]
                weights.append(scaled * along_y[j][count + start : count + start + 8, :])
                weights.append(scaled * along_z[count * j + start : count * j + start + 8, size_z:])
                for i, weight in enumerate(weights):
                    coef[i, x + j, rows, :] = weight
        return carry

    lax.fori_loop(0, planes // group, some, 0)


def advance_planes(cur, old, coef, bands, row_lo, row_hi, x, group):
    count, size_z = cur.shape[1:]
    along_z, along_y = differences(cur, x + 2, group, bands)
    for start in range(row_lo, row_hi, 8):
        rows = slice(start, start + 8)
        stack = [cur[x + k, rows, :] for k in range(group + 4)]
        for j in range(group):
            terms = [coef[i, x + j, rows, :] * stack[j + 2 + k] for i, k in enumerate(REACH)]
            block = along_z[count * j + start : count * j + start + 8, :]
            curved, sloped = along_y[j][rows, :], along_y[j][count + start : count + start + 8, :]
            even = coef[4, x + j, rows, :] * (block[:, :size_z] + curved)
            odd = coef[5, x + j, rows, :] * sloped + coef[6, x + j, rows, :] * block[:, size_z:]
            base = (stack[j + 2] + stack[j + 2]) - old[x + j + 2, rows, :]
            old[x + j + 2, rows, :] = (base + (even + odd)) + ((terms[0] + terms[1]) + (terms[2] + terms[3]))


def advance(cur, old, coef, bands, row_lo, row_hi, total):
    group = min(GROUP, total)
    body = min(2 * group, total)

    def some(g, carry):
        for first in range(0, body, group):
            advance_planes(cur, old, coef, bands, row_lo, row_hi, g * body + first, group)
        return carry

    if body == total:
        some(0, 0)
    else:
        lax.fori_loop(0, total // body, some, 0)


def inject(ref, cell, amplitude, first_row, rows, size_y):
    size_z = ref.shape[2]
    x = cell // (size_y * size_z)
    row = (cell // size_z) % size_y - first_row
    z = cell % size_z

    @pl.when((row >= 0) & (row < rows))
    def _():
        base = pl.multiple_of((row // 8) * 8, 8)
        lane = lax.broadcasted_iota(jnp.int32, (8, size_z), 1)
        sub = lax.broadcasted_iota(jnp.int32, (8, size_z), 0)
        hit = (lane == z) & (sub == row - base)
        where = (x + 2, pl.ds(base, 8), slice(None))
        ref[where] = ref[where] + jnp.where(hit, amplitude, 0.0)


def clear_edges(refs, rows):
    for ref in refs:
        planes, count, size_z = ref.shape
        for x in (0, 1, planes - 2, planes - 1):
            ref[x, :, :] = jnp.zeros((count, size_z), jnp.float32)
        if rows < count:
            ref[:, rows:, :] = jnp.zeros((planes, count - rows, size_z), jnp.float32)


def span(step, steps, rows):
    low, high = 2 * (step + 1), rows - 2 * (step + 1)
    return low // 8 * 8, min(rows, -(-high // 8) * 8)


def pack_body(dims, ids, now, old, courant, logb, *refs):
    slabs, planes, size_y, size_z, share, halo = dims
    outs, wide = refs[:-1], refs[-1]
    window = share + 2 * halo
    half = planes // 2
    slab, core = ids[0], ids[1]
    wide[:, :, 0:halo, :] = jnp.zeros((4, planes, halo, size_z), jnp.float32)
    wide[:, :, halo + size_y :, :] = jnp.zeros((4, planes, halo, size_z), jnp.float32)
    for i, ref in enumerate((courant, logb, now, old)):
        wide[i, :, halo : halo + size_y, :] = ref[...]
    for d in range(slabs):
        first = pl.multiple_of((slab ^ d) * share, 8)
        model, state = outs[2 * d], outs[2 * d + 1]
        for i in range(2):
            if d == 0:
                model[i * planes : (i + 1) * planes] = wide[i, :, pl.ds(first, window), :]
            else:
                model[i * half : (i + 1) * half] = wide[i, pl.ds(half * core, half), pl.ds(first, window), :]
            state[i * planes : (i + 1) * planes] = wide[2 + i, :, pl.ds(first, window), :]


def field_body(dims, ids, cells, traces, *refs):
    slabs, planes, size_y, size_z, share, halo, steps = dims
    window = share + 2 * halo
    half = planes // 2
    total = planes * slabs
    models, states, others = refs[:slabs], refs[slabs : 2 * slabs], refs[2 * slabs : 3 * slabs - 1]
    outs = refs[3 * slabs - 1 : 4 * slabs - 1]
    now, old, c_ref, b_ref, coef, *bands = refs[4 * slabs - 1 :]
    slab, core = ids[0], ids[1]
    clear_edges((now, old, c_ref, b_ref), window)
    fill_bands(*bands)
    inner = slice(0, window)
    for d in range(slabs):
        base = (slab ^ d) * planes + 2
        now[pl.ds(base, planes), inner, :] = states[d][:planes]
        old[pl.ds(base, planes), inner, :] = states[d][planes:]
        for i, ref in enumerate((c_ref, b_ref)):
            if d == 0:
                ref[pl.ds(base, planes), inner, :] = models[0][i * planes : (i + 1) * planes]
            else:
                ref[pl.ds(base + half * core, half), inner, :] = models[d][i * half : (i + 1) * half]
                ref[pl.ds(base + half * (1 - core), half), inner, :] = others[d - 1][i * half : (i + 1) * half]
    prepare(c_ref, b_ref, coef, bands, total)
    first = slab * share - halo
    for step in range(steps):
        low, high = span(step, steps, window)
        advance(now, old, coef, bands, low, high, total)
        inject(old, cells[0], traces[0, step], first, window, size_y)
        now, old = old, now
    for d in range(slabs):
        outs[d][...] = now[pl.ds((slab ^ d) * planes + 2, planes), halo : halo + share, :]


def sub_rows(tile, halo):
    return 2 * halo + (tile if tile % 8 == 0 else 2 * tile)


def sum_body(dims, ids, order, cells, traces, *refs):
    slabs, planes, size_y, size_z, tile, halo, steps, groups = dims
    window = sub_rows(tile, halo)
    half = planes // 2
    total = planes * slabs
    mine, others, snaps = refs[:slabs], refs[slabs : 2 * slabs], refs[2 * slabs]
    out = refs[2 * slabs + 1]
    now, old, c_ref, b_ref, coef, *bands = refs[2 * slabs + 2 :]
    slab, core, chip = ids[0], ids[1], ids[2]
    clear_edges((now, old, c_ref, b_ref), window)
    fill_bands(*bands)
    inner = slice(0, window)
    offset = pl.multiple_of(core * tile, 8) if tile % 8 == 0 else 0
    taken = pl.ds(offset, window)
    for d in range(slabs):
        base = (slab ^ d) * planes + 2
        for i, ref in enumerate((now, old, c_ref, b_ref)):
            ref[pl.ds(base + half * core, half), inner, :] = mine[d][i * half : (i + 1) * half, taken, :]
            ref[pl.ds(base + half * (1 - core), half), inner, :] = others[d][i * half : (i + 1) * half, taken, :]
    prepare(c_ref, b_ref, coef, bands, total)
    first = chip * 2 * tile - halo + offset
    acc = jnp.zeros((planes, tile, size_z), jnp.float32)
    for step in range(steps):
        low, high = span(step, steps, window)
        if step == steps - 1:
            advance_planes(now, old, coef, bands, low, high, slab * planes, planes)
        else:
            advance(now, old, coef, bands, low, high, total)

        def add(r, carry, target=old, step=step):
            inject(target, cells[r], traces[r, step], first, window, size_y)
            return carry

        lax.fori_loop(0, 2 * groups, add, 0)
        now, old = old, now
        if step % 2 == 1:
            slot = order[step // 2]
            piece = ((slot // 2) ^ chip) * 2 + ((slot % 2) ^ core)
            own = pl.ds(slab * planes + 2, planes)
            top = halo
            field = now[own, top : top + tile, :]
            if tile % 8:
                field = jnp.where(core == 0, field, now[own, top + tile : top + 2 * tile, :])
            acc = acc + field * snaps[piece]
    out[...] = acc


def unpack_body(dims, ids, *refs):
    slabs, share = dims
    out = refs[slabs]
    for d in range(slabs):
        out[:, pl.ds(pl.multiple_of((ids[0] ^ d) * share, 8), share), :] = refs[d][...]


def local(
    adjoint_now,
    adjoint_before,
    courant_field,
    log_buoyancy,
    snapshot_store,
    owner_order,
    receiver_cells,
    receiver_traces,
    residual_weights,
):
    planes, size_y, size_z = courant_field.shape
    steps = receiver_traces.shape[1]
    slabs, ranks = lax.axis_size("slab"), lax.axis_size("rcv")
    chips = ranks // 2
    halo = 2 * steps
    share = size_y // slabs
    tile = size_y // ranks
    half = planes // 2
    window = share + 2 * halo
    wide = 2 * tile + 2 * halo
    total = planes * slabs
    slab = lax.axis_index("slab")
    rank = lax.axis_index("rcv")
    core, chip = rank % 2, rank // 2
    ids = jnp.stack([slab, core, chip]).astype(jnp.int32)
    now, old, store = adjoint_now[0], adjoint_before[0], snapshot_store[0]

    shapes = []
    for d in range(slabs):
        shapes += [((2 * planes if d == 0 else 2 * half), window, size_z), (2 * planes, window, size_z)]
    packed = call(
        functools.partial(pack_body, (slabs, planes, size_y, size_z, share, halo)),
        shapes,
        [now, old, courant_field, log_buoyancy],
        [ids],
        [pltpu.VMEM((4, planes, size_y + 2 * halo, size_z), jnp.float32)],
        "pack",
    )
    models = [packed[0]] + [swap(packed[2 * d], "slab", d) for d in range(1, slabs)]
    states = [packed[1]] + [swap(packed[2 * d + 1], "slab", d) for d in range(1, slabs)]
    others = [swap(models[d], "rcv", 1) for d in range(1, slabs)]

    fields = residual_weights[0] * jnp.stack([now, old])
    fields = fields.reshape(2, 2, half, size_y, size_z)
    pick = functools.partial(lax.dynamic_index_in_dim, keepdims=False)
    tiles = store.reshape(planes, chips, 2, tile, size_z)
    row = jnp.concatenate([receiver_cells.astype(jnp.float32), residual_weights[0] * receiver_traces[0]])
    row = jnp.pad(row, (0, size_z - row.shape[0]))
    info = jnp.where(lax.broadcasted_iota(jnp.int32, (8, 1), 0) == core, row[None], 0.0)
    flat = lambda a: a.reshape(-1, size_z)
    sent = jnp.concatenate([flat(pick(fields, 1 - core, 1)), flat(pick(tiles, 1 - core, 2)), info])
    got = swap(sent, "rcv", 1)
    cut = 2 * half * size_y
    pair = pick(fields, core, 1) + got[:cut].reshape(2, half, size_y, size_z)
    pair = jnp.pad(pair, ((0, 0), (0, 0), (halo, halo), (0, 0)))
    tiles = jnp.stack([pick(tiles, core, 2), got[cut:-8].reshape(planes, chips, tile, size_z)])
    info = info + got[-8:]
    received = []
    for d in range(chips):
        to = chip ^ d
        rows = lax.dynamic_slice_in_dim(pair, to * 2 * tile, wide, 2)
        block = jnp.concatenate([flat(rows), flat(pick(tiles, to, 2)), info])
        received.append(swap(block, "rcv", 2 * d) if d else block)
    cut = 2 * half * wide
    summed = functools.reduce(jnp.add, [b[:cut] for b in received]).reshape(2 * half, wide, size_z)
    snaps = jnp.stack([b[cut:-8].reshape(2, planes, tile, size_z) for b in received])
    snaps = snaps.reshape(2 * chips, planes, tile, size_z)
    infos = jnp.concatenate([b[-8:-6] for b in received])
    all_cells = infos[:, 0].astype(jnp.int32)
    all_traces = infos[:, 1 : 1 + steps]

    model = jnp.stack([courant_field, log_buoyancy])
    model = lax.dynamic_slice_in_dim(model, half * core, half, 1)
    model = jnp.pad(model, ((0, 0), (0, 0), (halo, halo), (0, 0)))
    model = lax.dynamic_slice_in_dim(model, chip * 2 * tile, wide, 2)
    block = jnp.concatenate([summed, model.reshape(2 * half, wide, size_z)])
    mine = [block] + [swap(block, "slab", d) for d in range(1, slabs)]
    theirs = [swap(b, "rcv", 1) for b in mine]

    def scratch(rows):
        rows = -(-rows // 16) * 16
        return (
            [pltpu.VMEM((total + 4, rows, size_z), jnp.float32)] * 4
            + [pltpu.VMEM((7, total, rows, size_z), jnp.float32)]
            + [pltpu.VMEM((2 * size_z, 2 * size_z), jnp.bfloat16), pltpu.VMEM((2 * rows, 2 * rows), jnp.bfloat16)]
        )

    finals = call(
        functools.partial(field_body, (slabs, planes, size_y, size_z, share, halo, steps)),
        [(planes, share, size_z)] * slabs,
        models + states + others,
        [ids, receiver_cells, receiver_traces],
        scratch(window),
        "field",
        flops=40 * steps * total * window * size_z,
    )
    back = [finals[0]] + [swap(finals[d], "slab", d) for d in range(1, slabs)]
    (sensitivity,) = call(
        functools.partial(sum_body, (slabs, planes, size_y, size_z, tile, halo, steps, chips)),
        [(planes, tile, size_z)],
        mine + theirs + [snaps],
        [ids, owner_order, all_cells, all_traces],
        scratch(sub_rows(tile, halo)),
        "summed",
        flops=40 * steps * total * sub_rows(tile, halo) * size_z,
    )
    (after,) = call(
        functools.partial(unpack_body, (slabs, share)),
        [(planes, size_y, size_z)],
        back,
        [ids],
        [],
        "unpack",
    )
    return (sensitivity, after[None])


def solution(mesh):
    placed = (
        P("rcv", "slab", None, None),
        P("rcv", "slab", None, None),
        P("slab", None, None),
        P("slab", None, None),
        P("rcv", "slab", None, None),
        P(),
        P("rcv"),
        P("rcv", None),
        P("rcv"),
    )
    return jax.shard_map(
        local,
        mesh=mesh,
        in_specs=placed,
        out_specs=(P("slab", "rcv", None), P("rcv", "slab", None, None)),
        check_vma=False,
    )
```

```python
import functools

import jax
import jax.numpy as jnp
from jax import lax
from jax.experimental import pallas as pl
from jax.experimental.pallas import tpu as pltpu
from jax.sharding import PartitionSpec as P


REACH = (1, -1, 2, -2)
GROUP = 8


VMEM = pl.BlockSpec(memory_space=pltpu.VMEM)
SMEM = pl.BlockSpec(memory_space=pltpu.SMEM)


def swap(block, axis, mask):
    peers = lax.axis_size(axis)
    return lax.ppermute(block, axis, [(i, i ^ mask) for i in range(peers)])


def call(body, outs, inputs, scalars, scratch, flops=0):
    size = sum(x.size * 4 for x in inputs) + sum(4 * functools.reduce(lambda a, b: a * b, o) for o in outs)
    return pl.pallas_call(
        body,
        out_shape=[jax.ShapeDtypeStruct(o, jnp.float32) for o in outs],
        in_specs=[SMEM] * len(scalars) + [VMEM] * len(inputs),
        out_specs=[VMEM] * len(outs),
        scratch_shapes=scratch,
        cost_estimate=pl.CostEstimate(flops=flops, bytes_accessed=size, transcendentals=0),
    )(*scalars, *inputs)


def band(gap, near, far, centre):
    apart = jnp.abs(gap)
    weight = jnp.where(apart == 1, near, jnp.where(apart == 2, far, 0.0))
    if centre is None:
        return jnp.where(gap < 0, -weight, weight)
    return jnp.where(apart == 0, centre, weight)


def fill_bands(lanes, rows):
    size = lanes.shape[0] // 2
    gap = lax.broadcasted_iota(jnp.int32, lanes.shape, 0) % size - lax.broadcasted_iota(jnp.int32, lanes.shape, 1) % size
    column = lax.broadcasted_iota(jnp.int32, lanes.shape, 1)
    lanes[...] = jnp.where(column < size, band(gap, 16.0, -1.0, -90.0), band(gap, 8.0, -1.0, None)).astype(jnp.bfloat16)
    size = rows.shape[0] // 2
    gap = lax.broadcasted_iota(jnp.int32, rows.shape, 1) % size - lax.broadcasted_iota(jnp.int32, rows.shape, 0) % size
    row = lax.broadcasted_iota(jnp.int32, rows.shape, 0)
    rows[...] = jnp.where(row < size, band(gap, 16.0, -1.0, 0.0), band(gap, 8.0, -1.0, None)).astype(jnp.bfloat16)


def differences(ref, x, group, bands):
    lanes, rows = bands
    _, size_z = ref.shape[1:]
    parts = []
    for j in range(group):
        field = ref[x + j]
        high = field.astype(jnp.bfloat16)
        low = (field - high.astype(jnp.float32)).astype(jnp.bfloat16)
        parts.append((high, low))
    flat = jnp.concatenate([jnp.concatenate(p, axis=1) for p in parts], axis=0)
    along_z = jnp.dot(flat, lanes[...], preferred_element_type=jnp.float32)
    along_y = []
    for j in range(0, group, 2):
        pair = jnp.concatenate([jnp.concatenate(p, axis=0) for p in parts[j : j + 2]], axis=1)
        both = jnp.dot(rows[...], pair, preferred_element_type=jnp.float32)
        along_y += [both[:, i * size_z : (i + 1) * size_z] for i in range(2)]
    return along_z, along_y


def prepare(c_ref, b_ref, coef, bands, planes):
    count, size_z = b_ref.shape[1:]
    group = min(GROUP, planes)

    def some(g, carry):
        x = g * group
        along_z, along_y = differences(b_ref, x + 2, group, bands)
        for start in range(0, count, 8):
            rows = slice(start, start + 8)
            stack = [b_ref[x + k, rows, :] for k in range(group + 4)]
            for j in range(group):
                c = c_ref[x + j + 2, rows, :]
                scaled = (1.0 / 144.0) * c
                twelfth = (1.0 / 12.0) * c
                near = 16.0 * twelfth
                p1, m1, p2, m2 = [stack[j + 2 + k] for k in REACH]
                slope = scaled * (8.0 * (p1 - m1) - (p2 - m2))
                steep = 8.0 * slope
                weights = [near + steep, near - steep, -twelfth - slope, slope - twelfth, twelfth]
                weights.append(scaled * along_y[j][count + start : count + start + 8, :])
                weights.append(scaled * along_z[count * j + start : count * j + start + 8, size_z:])
                for i, weight in enumerate(weights):
                    coef[i, x + j, rows, :] = weight
        return carry

    lax.fori_loop(0, planes // group, some, 0)


def advance_planes(cur, old, coef, bands, row_lo, row_hi, x, group):
    count, size_z = cur.shape[1:]
    along_z, along_y = differences(cur, x + 2, group, bands)
    for start in range(row_lo, row_hi, 8):
        rows = slice(start, start + 8)
        stack = [cur[x + k, rows, :] for k in range(group + 4)]
        for j in range(group):
            terms = [coef[i, x + j, rows, :] * stack[j + 2 + k] for i, k in enumerate(REACH)]
            block = along_z[count * j + start : count * j + start + 8, :]
            curved, sloped = along_y[j][rows, :], along_y[j][count + start : count + start + 8, :]
            even = coef[4, x + j, rows, :] * (block[:, :size_z] + curved)
            odd = coef[5, x + j, rows, :] * sloped + coef[6, x + j, rows, :] * block[:, size_z:]
            base = (stack[j + 2] + stack[j + 2]) - old[x + j + 2, rows, :]
            old[x + j + 2, rows, :] = (base + (even + odd)) + ((terms[0] + terms[1]) + (terms[2] + terms[3]))


def advance(cur, old, coef, bands, row_lo, row_hi, total):
    group = min(GROUP, total)
    body = min(2 * group, total)

    def some(g, carry):
        for first in range(0, body, group):
            advance_planes(cur, old, coef, bands, row_lo, row_hi, g * body + first, group)
        return carry

    if body == total:
        some(0, 0)
    else:
        lax.fori_loop(0, total // body, some, 0)


def place(cell, first_row, size_y, size_z):
    return cell // (size_y * size_z), (cell // size_z) % size_y - first_row, cell % size_z


def inject(ref, spot, amplitude):
    x, row, z = spot
    size_z = ref.shape[2]
    base = pl.multiple_of((row // 8) * 8, 8)
    lane = lax.broadcasted_iota(jnp.int32, (8, size_z), 1)
    sub = lax.broadcasted_iota(jnp.int32, (8, size_z), 0)
    hit = (lane == z) & (sub == row - base)
    where = (x + 2, pl.ds(base, 8), slice(None))
    ref[where] = ref[where] + jnp.where(hit, amplitude, 0.0)


def clear_edges(refs, rows):
    for ref in refs:
        planes, count, size_z = ref.shape
        for x in (0, 1, planes - 2, planes - 1):
            ref[x, :, :] = jnp.zeros((count, size_z), jnp.float32)
        if rows < count:
            ref[:, rows:, :] = jnp.zeros((planes, count - rows, size_z), jnp.float32)


def span(step, rows):
    low, high = 2 * (step + 1), rows - 2 * (step + 1)
    return low // 8 * 8, min(rows, -(-high // 8) * 8)


def weigh_body(dims, ids, cells, traces, weights, now, old, own, sent):
    half, size_y, size_z, steps = dims
    core, weight = ids[1], weights[0]
    for i, ref in enumerate((now, old)):
        for j in range(half):
            own[i, j] = weight * ref[half * core + j]
            sent[pl.ds((i * half + j) * size_y, size_y), :] = weight * ref[half * (1 - core) + j]
    lane = lax.broadcasted_iota(jnp.int32, (8, size_z), 1)
    sub = lax.broadcasted_iota(jnp.int32, (8, size_z), 0)
    row = jnp.where(lane == 0, cells[0].astype(jnp.float32), 0.0)
    for step in range(steps):
        row = jnp.where(lane == 1 + step, weight * traces[0, step], row)
    sent[pl.ds(2 * half * size_y, 8), :] = jnp.where(sub == core, row, 0.0)


def pack_body(dims, ids, now, old, courant, logb, *refs):
    slabs, planes, size_y, size_z, share, halo = dims
    outs, wide = refs[:-1], refs[-1]
    window = share + 2 * halo
    half = planes // 2
    slab, core = ids[0], ids[1]
    wide[:, :, 0:halo, :] = jnp.zeros((4, planes, halo, size_z), jnp.float32)
    wide[:, :, halo + size_y :, :] = jnp.zeros((4, planes, halo, size_z), jnp.float32)
    for i, ref in enumerate((courant, logb, now, old)):
        wide[i, :, halo : halo + size_y, :] = ref[...]
    for d in range(slabs):
        first = pl.multiple_of((slab ^ d) * share, 8)
        model, state = outs[2 * d], outs[2 * d + 1]
        for i in range(2):
            if d == 0:
                model[i * planes : (i + 1) * planes] = wide[i, :, pl.ds(first, window), :]
            else:
                model[i * half : (i + 1) * half] = wide[i, pl.ds(half * core, half), pl.ds(first, window), :]
            state[i * planes : (i + 1) * planes] = wide[2 + i, :, pl.ds(first, window), :]


def field_body(dims, ids, cells, traces, *refs):
    slabs, planes, size_y, size_z, share, halo, steps = dims
    window = share + 2 * halo
    half = planes // 2
    total = planes * slabs
    models, states, others = refs[:slabs], refs[slabs : 2 * slabs], refs[2 * slabs : 3 * slabs - 1]
    outs = refs[3 * slabs - 1 : 4 * slabs - 1]
    now, old, c_ref, b_ref, coef, *bands = refs[4 * slabs - 1 :]
    slab, core = ids[0], ids[1]
    clear_edges((now, old, c_ref, b_ref), window)
    fill_bands(*bands)
    inner = slice(0, window)
    for d in range(slabs):
        base = (slab ^ d) * planes + 2
        now[pl.ds(base, planes), inner, :] = states[d][:planes]
        old[pl.ds(base, planes), inner, :] = states[d][planes:]
        for i, ref in enumerate((c_ref, b_ref)):
            if d == 0:
                ref[pl.ds(base, planes), inner, :] = models[0][i * planes : (i + 1) * planes]
            else:
                ref[pl.ds(base + half * core, half), inner, :] = models[d][i * half : (i + 1) * half]
                ref[pl.ds(base + half * (1 - core), half), inner, :] = others[d - 1][i * half : (i + 1) * half]
    prepare(c_ref, b_ref, coef, bands, total)
    spot = place(cells[0], slab * share - halo, size_y, size_z)
    for step in range(steps):
        low, high = span(step, window)
        advance(now, old, coef, bands, low, high, total)

        @pl.when((spot[1] >= 0) & (spot[1] < window))
        def _(target=old, step=step):
            inject(target, spot, traces[0, step])

        now, old = old, now
    for d in range(slabs):
        outs[d][...] = now[pl.ds((slab ^ d) * planes + 2, planes), halo : halo + share, :]


def sub_rows(tile, halo):
    return 2 * halo + (tile if tile % 8 == 0 else 2 * tile)


def sum_body(dims, ids, order, cells, traces, *refs):
    slabs, planes, size_y, size_z, tile, halo, steps, groups = dims
    window = sub_rows(tile, halo)
    half = planes // 2
    total = planes * slabs
    mine, others, snaps = refs[:slabs], refs[slabs : 2 * slabs], refs[2 * slabs]
    out = refs[2 * slabs + 1]
    spots, now, old, c_ref, b_ref, coef, *bands = refs[2 * slabs + 2 :]
    slab, core, chip = ids[0], ids[1], ids[2]
    clear_edges((now, old, c_ref, b_ref), window)
    fill_bands(*bands)
    inner = slice(0, window)
    offset = pl.multiple_of(core * tile, 8) if tile % 8 == 0 else 0
    taken = pl.ds(offset, window)
    for d in range(slabs):
        base = (slab ^ d) * planes + 2
        for i, ref in enumerate((now, old, c_ref, b_ref)):
            ref[pl.ds(base + half * core, half), inner, :] = mine[d][i * half : (i + 1) * half, taken, :]
            ref[pl.ds(base + half * (1 - core), half), inner, :] = others[d][i * half : (i + 1) * half, taken, :]
    prepare(c_ref, b_ref, coef, bands, total)
    first = chip * 2 * tile - halo + offset

    def note(r, found):
        spot = place(cells[r], first, size_y, size_z)
        for i, value in enumerate(spot + (r,)):
            spots[i, found] = value
        return found + ((spot[1] >= 0) & (spot[1] < window)).astype(jnp.int32)

    inside = lax.fori_loop(0, 2 * groups, note, 0)
    acc = jnp.zeros((planes, tile, size_z), jnp.float32)
    for step in range(steps):
        low, high = span(step, window)
        if step == steps - 1:
            advance_planes(now, old, coef, bands, low, high, slab * planes, planes)
        else:
            advance(now, old, coef, bands, low, high, total)

        def add(i, carry, target=old, step=step):
            inject(target, (spots[0, i], spots[1, i], spots[2, i]), traces[spots[3, i], step])
            return carry

        lax.fori_loop(0, inside, add, 0)
        now, old = old, now
        if step % 2 == 1:
            slot = order[step // 2]
            piece = ((slot // 2) ^ chip) * 2 + ((slot % 2) ^ core)
            own = pl.ds(slab * planes + 2, planes)
            top = halo
            field = now[own, top : top + tile, :]
            if tile % 8:
                field = jnp.where(core == 0, field, now[own, top + tile : top + 2 * tile, :])
            acc = acc + field * snaps[piece]
    out[...] = acc


def unpack_body(dims, ids, *refs):
    slabs, share = dims
    out = refs[slabs]
    for d in range(slabs):
        out[:, pl.ds(pl.multiple_of((ids[0] ^ d) * share, 8), share), :] = refs[d][...]


def local(
    adjoint_now,
    adjoint_before,
    courant_field,
    log_buoyancy,
    snapshot_store,
    owner_order,
    receiver_cells,
    receiver_traces,
    residual_weights,
):
    planes, size_y, size_z = courant_field.shape
    steps = receiver_traces.shape[1]
    slabs, ranks = lax.axis_size("slab"), lax.axis_size("rcv")
    chips = ranks // 2
    halo = 2 * steps
    share = size_y // slabs
    tile = size_y // ranks
    half = planes // 2
    window = share + 2 * halo
    wide = 2 * tile + 2 * halo
    total = planes * slabs
    slab = lax.axis_index("slab")
    rank = lax.axis_index("rcv")
    core, chip = rank % 2, rank // 2
    ids = jnp.stack([slab, core, chip]).astype(jnp.int32)
    now, old, store = adjoint_now[0], adjoint_before[0], snapshot_store[0]

    cut = 2 * half * size_y
    own, sent = call(
        functools.partial(weigh_body, (half, size_y, size_z, steps)),
        [(2, half, size_y, size_z), (cut + 8, size_z)],
        [now, old],
        [ids, receiver_cells, receiver_traces, residual_weights],
        [],
    )
    got = swap(sent, "rcv", 1)

    shapes = []
    for d in range(slabs):
        shapes += [((2 * planes if d == 0 else 2 * half), window, size_z), (2 * planes, window, size_z)]
    packed = call(
        functools.partial(pack_body, (slabs, planes, size_y, size_z, share, halo)),
        shapes,
        [now, old, courant_field, log_buoyancy],
        [ids],
        [pltpu.VMEM((4, planes, size_y + 2 * halo, size_z), jnp.float32)],
    )
    models = [packed[0]] + [swap(packed[2 * d], "slab", d) for d in range(1, slabs)]
    states = [packed[1]] + [swap(packed[2 * d + 1], "slab", d) for d in range(1, slabs)]
    others = [swap(models[d], "rcv", 1) for d in range(1, slabs)]

    flat = lambda a: a.reshape(-1, size_z)
    pair = own + got[:cut].reshape(2, half, size_y, size_z)
    pair = jnp.pad(pair, ((0, 0), (0, 0), (halo, halo), (0, 0)))
    info = sent[cut:] + got[cut:]
    received = []
    for d in range(chips):
        rows = lax.dynamic_slice_in_dim(pair, (chip ^ d) * 2 * tile, wide, 2)
        block = jnp.concatenate([flat(rows), info])
        received.append(swap(block, "rcv", 2 * d) if d else block)
    cut = 2 * half * wide
    summed = functools.reduce(jnp.add, [b[:cut] for b in received]).reshape(2 * half, wide, size_z)
    infos = jnp.concatenate([b[cut : cut + 2] for b in received])
    all_cells = infos[:, 0].astype(jnp.int32)
    all_traces = infos[:, 1 : 1 + steps]

    pick = functools.partial(lax.dynamic_index_in_dim, keepdims=False)
    tiles, _ = lax.optimization_barrier((store.reshape(planes, chips, 2, tile, size_z), got))
    tiles = jnp.stack([pick(tiles, core, 2), swap(pick(tiles, 1 - core, 2), "rcv", 1)])
    snaps = [pick(tiles, chip ^ d, 2) for d in range(chips)]
    snaps = jnp.concatenate([snaps[0]] + [swap(snaps[d], "rcv", 2 * d) for d in range(1, chips)])

    model = jnp.stack([courant_field, log_buoyancy])
    model = lax.dynamic_slice_in_dim(model, half * core, half, 1)
    model = jnp.pad(model, ((0, 0), (0, 0), (halo, halo), (0, 0)))
    model = lax.dynamic_slice_in_dim(model, chip * 2 * tile, wide, 2)
    block = jnp.concatenate([summed, model.reshape(2 * half, wide, size_z)])
    mine = [block] + [swap(block, "slab", d) for d in range(1, slabs)]

    def scratch(rows):
        rows = -(-rows // 16) * 16
        return (
            [pltpu.VMEM((total + 4, rows, size_z), jnp.float32)] * 4
            + [pltpu.VMEM((7, total, rows, size_z), jnp.float32)]
            + [pltpu.VMEM((2 * size_z, 2 * size_z), jnp.bfloat16), pltpu.VMEM((2 * rows, 2 * rows), jnp.bfloat16)]
        )

    finals = call(
        functools.partial(field_body, (slabs, planes, size_y, size_z, share, halo, steps)),
        [(planes, share, size_z)] * slabs,
        models + states + others,
        [ids, receiver_cells, receiver_traces],
        scratch(window),
        flops=40 * steps * total * window * size_z,
    )
    mine[1:] = lax.optimization_barrier(tuple(mine[1:]) + tuple(finals))[: slabs - 1]
    back = [finals[0]] + [swap(finals[d], "slab", d) for d in range(1, slabs)]
    theirs = [swap(b, "rcv", 1) for b in mine]
    (sensitivity,) = call(
        functools.partial(sum_body, (slabs, planes, size_y, size_z, tile, halo, steps, chips)),
        [(planes, tile, size_z)],
        mine + theirs + [snaps],
        [ids, owner_order, all_cells, all_traces],
        [pltpu.SMEM((4, 2 * chips + 1), jnp.int32)] + scratch(sub_rows(tile, halo)),
        flops=40 * steps * total * sub_rows(tile, halo) * size_z,
    )
    (after,) = call(functools.partial(unpack_body, (slabs, share)), [(planes, size_y, size_z)], back, [ids], [])
    return (sensitivity, after[None])


def solution(mesh):
    placed = (
        P("rcv", "slab", None, None),
        P("rcv", "slab", None, None),
        P("slab", None, None),
        P("slab", None, None),
        P("rcv", "slab", None, None),
        P(),
        P("rcv"),
        P("rcv", None),
        P("rcv"),
    )

    return jax.shard_map(
        local,
        mesh=mesh,
        in_specs=placed,
        out_specs=(P("slab", "rcv", None), P("rcv", "slab", None, None)),
        check_vma=False,
    )
```

```python
import functools

import jax
import jax.numpy as jnp
from jax import lax
from jax.experimental import pallas as pl
from jax.experimental.pallas import tpu as pltpu
from jax.sharding import PartitionSpec as P


REACH = (1, -1, 2, -2)
GROUP = 8
SPARE = 4 << 20


VMEM = pl.BlockSpec(memory_space=pltpu.VMEM)
SMEM = pl.BlockSpec(memory_space=pltpu.SMEM)


def swap(block, axis, mask):
    peers = lax.axis_size(axis)
    return lax.ppermute(block, axis, [(i, i ^ mask) for i in range(peers)])


def count(shape):
    return functools.reduce(lambda a, b: a * b, shape)


def call(body, outs, inputs, scalars, scratch, flops=0):
    size = 4 * (sum(x.size for x in inputs) + sum(count(o) for o in outs))
    held = sum(count(s.shape) * 4 for s in scratch)
    return pl.pallas_call(
        body,
        out_shape=[jax.ShapeDtypeStruct(o, jnp.float32) for o in outs],
        in_specs=[SMEM] * len(scalars) + [VMEM] * len(inputs),
        out_specs=[VMEM] * len(outs),
        scratch_shapes=scratch,
        cost_estimate=pl.CostEstimate(flops=flops, bytes_accessed=size, transcendentals=0),
        compiler_params=pltpu.CompilerParams(vmem_limit_bytes=size + held + SPARE),
    )(*scalars, *inputs)


def position():
    rank = lax.axis_index("rcv")
    return lax.axis_index("slab"), rank % 2, rank // 2


def band(gap, near, far, centre):
    apart = jnp.abs(gap)
    weight = jnp.where(apart == 1, near, jnp.where(apart == 2, far, 0.0))
    if centre is None:
        return jnp.where(gap < 0, -weight, weight)
    return jnp.where(apart == 0, centre, weight)


def fill_bands(lanes, rows):
    size = lanes.shape[0] // 2
    gap = lax.broadcasted_iota(jnp.int32, lanes.shape, 0) % size - lax.broadcasted_iota(jnp.int32, lanes.shape, 1) % size
    column = lax.broadcasted_iota(jnp.int32, lanes.shape, 1)
    lanes[...] = jnp.where(column < size, band(gap, 16.0, -1.0, -90.0), band(gap, 8.0, -1.0, None)).astype(jnp.bfloat16)
    size = rows.shape[0] // 2
    gap = lax.broadcasted_iota(jnp.int32, rows.shape, 1) % size - lax.broadcasted_iota(jnp.int32, rows.shape, 0) % size
    row = lax.broadcasted_iota(jnp.int32, rows.shape, 0)
    rows[...] = jnp.where(row < size, band(gap, 16.0, -1.0, 0.0), band(gap, 8.0, -1.0, None)).astype(jnp.bfloat16)


def differences(ref, x, group, bands):
    lanes, rows = bands
    _, size_z = ref.shape[1:]
    parts = []
    for j in range(group):
        field = ref[x + j]
        high = field.astype(jnp.bfloat16)
        low = (field - high.astype(jnp.float32)).astype(jnp.bfloat16)
        parts.append((high, low))
    flat = jnp.concatenate([jnp.concatenate(p, axis=1) for p in parts], axis=0)
    along_z = jnp.dot(flat, lanes[...], preferred_element_type=jnp.float32)
    along_y = []
    for j in range(0, group, 2):
        pair = jnp.concatenate([jnp.concatenate(p, axis=0) for p in parts[j : j + 2]], axis=1)
        both = jnp.dot(rows[...], pair, preferred_element_type=jnp.float32)
        along_y += [both[:, i * size_z : (i + 1) * size_z] for i in range(2)]
    return along_z, along_y


def prepare(c_ref, b_ref, coef, bands, planes):
    count, size_z = b_ref.shape[1:]
    group = min(GROUP, planes)

    def some(g, carry):
        x = g * group
        along_z, along_y = differences(b_ref, x + 2, group, bands)
        for start in range(0, count, 8):
            rows = slice(start, start + 8)
            stack = [b_ref[x + k, rows, :] for k in range(group + 4)]
            for j in range(group):
                c = c_ref[x + j + 2, rows, :]
                scaled = (1.0 / 144.0) * c
                twelfth = (1.0 / 12.0) * c
                near = 16.0 * twelfth
                p1, m1, p2, m2 = [stack[j + 2 + k] for k in REACH]
                slope = scaled * (8.0 * (p1 - m1) - (p2 - m2))
                steep = 8.0 * slope
                weights = [near + steep, near - steep, -twelfth - slope, slope - twelfth, twelfth]
                weights.append(scaled * along_y[j][count + start : count + start + 8, :])
                weights.append(scaled * along_z[count * j + start : count * j + start + 8, size_z:])
                for i, weight in enumerate(weights):
                    coef[i, x + j, rows, :] = weight
        return carry

    lax.fori_loop(0, planes // group, some, 0)


def advance_planes(cur, old, coef, bands, row_lo, row_hi, x, group):
    count, size_z = cur.shape[1:]
    along_z, along_y = differences(cur, x + 2, group, bands)
    for start in range(row_lo, row_hi, 8):
        rows = slice(start, start + 8)
        stack = [cur[x + k, rows, :] for k in range(group + 4)]
        for j in range(group):
            terms = [coef[i, x + j, rows, :] * stack[j + 2 + k] for i, k in enumerate(REACH)]
            block = along_z[count * j + start : count * j + start + 8, :]
            curved, sloped = along_y[j][rows, :], along_y[j][count + start : count + start + 8, :]
            even = coef[4, x + j, rows, :] * (block[:, :size_z] + curved)
            odd = coef[5, x + j, rows, :] * sloped + coef[6, x + j, rows, :] * block[:, size_z:]
            base = (stack[j + 2] + stack[j + 2]) - old[x + j + 2, rows, :]
            old[x + j + 2, rows, :] = (base + (even + odd)) + ((terms[0] + terms[1]) + (terms[2] + terms[3]))


def advance(cur, old, coef, bands, row_lo, row_hi, total):
    group = min(GROUP, total)
    body = min(2 * group, total)

    def some(g, carry):
        for first in range(0, body, group):
            advance_planes(cur, old, coef, bands, row_lo, row_hi, g * body + first, group)
        return carry

    if body == total:
        some(0, 0)
    else:
        lax.fori_loop(0, total // body, some, 0)


def place(cell, first_row, size_y, size_z):
    return cell // (size_y * size_z), (cell // size_z) % size_y - first_row, cell % size_z


def inject(ref, spot, amplitude):
    x, row, z = spot
    size_z = ref.shape[2]
    base = pl.multiple_of((row // 8) * 8, 8)
    lane = lax.broadcasted_iota(jnp.int32, (8, size_z), 1)
    sub = lax.broadcasted_iota(jnp.int32, (8, size_z), 0)
    hit = (lane == z) & (sub == row - base)
    where = (x + 2, pl.ds(base, 8), slice(None))
    ref[where] = ref[where] + jnp.where(hit, amplitude, 0.0)


def clear_edges(refs, rows):
    for ref in refs:
        planes, count, size_z = ref.shape
        for x in (0, 1, planes - 2, planes - 1):
            ref[x, :, :] = jnp.zeros((count, size_z), jnp.float32)
        if rows < count:
            ref[:, rows:, :] = jnp.zeros((planes, count - rows, size_z), jnp.float32)


def span(step, rows):
    low, high = 2 * (step + 1), rows - 2 * (step + 1)
    return low // 8 * 8, min(rows, -(-high // 8) * 8)


def pack_body(dims, cells, traces, weights, now, old, courant, logb, *refs):
    slabs, planes, size_y, size_z, share, halo, steps = dims
    own, sent, whole, *outs, wide = refs
    window = share + 2 * halo
    half = planes // 2
    slab, core, _ = position()
    weight = weights[0]
    for i, ref in enumerate((now, old)):
        for j in range(half):
            own[i, j] = weight * ref[half * core + j]
            sent[pl.ds((i * half + j) * size_y, size_y), :] = weight * ref[half * (1 - core) + j]
    lane = lax.broadcasted_iota(jnp.int32, (8, size_z), 1)
    sub = lax.broadcasted_iota(jnp.int32, (8, size_z), 0)
    row = jnp.where(lane == 0, cells[0].astype(jnp.float32), 0.0)
    for step in range(steps):
        row = jnp.where(lane == 1 + step, weight * traces[0, step], row)
    sent[pl.ds(2 * half * size_y, 8), :] = jnp.where(sub == core, row, 0.0)
    wide[:, :, 0:halo, :] = jnp.zeros((4, planes, halo, size_z), jnp.float32)
    wide[:, :, halo + size_y :, :] = jnp.zeros((4, planes, halo, size_z), jnp.float32)
    for i, ref in enumerate((courant, logb, now, old)):
        wide[i, :, halo : halo + size_y, :] = ref[...]
    for d in range(slabs):
        rows = pl.ds(pl.multiple_of((slab ^ d) * share, 8), window)
        if d == 0:
            for i in range(4):
                whole[i * planes : (i + 1) * planes] = wide[i, :, rows, :]
            continue
        out = outs[d - 1]
        for i in range(2):
            out[i * half : (i + 1) * half] = wide[i, pl.ds(half * core, half), rows, :]
            out[2 * half + i * planes : 2 * half + (i + 1) * planes] = wide[2 + i, :, rows, :]


def field_body(dims, cells, traces, whole, *refs):
    slabs, planes, size_y, size_z, share, halo, steps = dims
    window = share + 2 * halo
    half = planes // 2
    total = planes * slabs
    blocks, others, outs = refs[: slabs - 1], refs[slabs - 1 : 2 * slabs - 2], refs[2 * slabs - 2 : 3 * slabs - 2]
    now, old, c_ref, b_ref, coef, *bands = refs[3 * slabs - 2 :]
    slab, core, _ = position()
    clear_edges((now, old, c_ref, b_ref), window)
    fill_bands(*bands)
    inner = slice(0, window)
    for d in range(slabs):
        base = (slab ^ d) * planes + 2
        if d == 0:
            for i, ref in enumerate((c_ref, b_ref, now, old)):
                ref[pl.ds(base, planes), inner, :] = whole[i * planes : (i + 1) * planes]
            continue
        for i, ref in enumerate((now, old)):
            first = 2 * half + i * planes
            ref[pl.ds(base, planes), inner, :] = blocks[d - 1][first : first + planes]
        for i, ref in enumerate((c_ref, b_ref)):
            ref[pl.ds(base + half * core, half), inner, :] = blocks[d - 1][i * half : (i + 1) * half]
            ref[pl.ds(base + half * (1 - core), half), inner, :] = others[d - 1][i * half : (i + 1) * half]
    prepare(c_ref, b_ref, coef, bands, total)
    spot = place(cells[0], slab * share - halo, size_y, size_z)
    for step in range(steps):
        low, high = span(step, window)
        advance(now, old, coef, bands, low, high, total)

        @pl.when((spot[1] >= 0) & (spot[1] < window))
        def _(target=old, step=step):
            inject(target, spot, traces[0, step])

        now, old = old, now
    for d in range(slabs):
        outs[d][...] = now[pl.ds((slab ^ d) * planes + 2, planes), halo : halo + share, :]


def sub_rows(tile, halo):
    return 2 * halo + (tile if tile % 8 == 0 else 2 * tile)


def sum_body(dims, order, cells, traces, *refs):
    slabs, planes, size_y, size_z, tile, halo, steps, groups = dims
    window = sub_rows(tile, halo)
    half = planes // 2
    total = planes * slabs
    mine, others, shots = refs[:slabs], refs[slabs : 2 * slabs], refs[2 * slabs : 2 * slabs + groups]
    out, spots, snaps, now, old, c_ref, b_ref, coef, *bands = refs[2 * slabs + groups :]
    slab, core, chip = position()
    for d in range(groups):
        snaps[2 * d : 2 * d + 2] = shots[d][...]
    clear_edges((now, old, c_ref, b_ref), window)
    fill_bands(*bands)
    inner = slice(0, window)
    offset = pl.multiple_of(core * tile, 8) if tile % 8 == 0 else 0
    taken = pl.ds(offset, window)
    for d in range(slabs):
        base = (slab ^ d) * planes + 2
        for i, ref in enumerate((now, old, c_ref, b_ref)):
            ref[pl.ds(base + half * core, half), inner, :] = mine[d][i * half : (i + 1) * half, taken, :]
            ref[pl.ds(base + half * (1 - core), half), inner, :] = others[d][i * half : (i + 1) * half, taken, :]
    prepare(c_ref, b_ref, coef, bands, total)
    first = chip * 2 * tile - halo + offset

    def note(r, found):
        spot = place(cells[r], first, size_y, size_z)
        for i, value in enumerate(spot + (r,)):
            spots[i, found] = value
        return found + ((spot[1] >= 0) & (spot[1] < window)).astype(jnp.int32)

    inside = lax.fori_loop(0, 2 * groups, note, 0)
    acc = jnp.zeros((planes, tile, size_z), jnp.float32)
    for step in range(steps):
        low, high = span(step, window)
        if step == steps - 1:
            advance_planes(now, old, coef, bands, low, high, slab * planes, planes)
        else:
            advance(now, old, coef, bands, low, high, total)

        def add(i, carry, target=old, step=step):
            inject(target, (spots[0, i], spots[1, i], spots[2, i]), traces[spots[3, i], step])
            return carry

        lax.fori_loop(0, inside, add, 0)
        now, old = old, now
        if step % 2 == 1:
            slot = order[step // 2]
            piece = ((slot // 2) ^ chip) * 2 + ((slot % 2) ^ core)
            own = pl.ds(slab * planes + 2, planes)
            top = halo
            field = now[own, top : top + tile, :]
            if tile % 8:
                field = jnp.where(core == 0, field, now[own, top + tile : top + 2 * tile, :])
            acc = acc + field * snaps[piece]
    out[...] = acc


def unpack_body(dims, *refs):
    slabs, share = dims
    out = refs[slabs]
    slab, _, _ = position()
    for d in range(slabs):
        out[:, pl.ds(pl.multiple_of((slab ^ d) * share, 8), share), :] = refs[d][...]


def local(
    adjoint_now,
    adjoint_before,
    courant_field,
    log_buoyancy,
    snapshot_store,
    owner_order,
    receiver_cells,
    receiver_traces,
    residual_weights,
):
    planes, size_y, size_z = courant_field.shape
    steps = receiver_traces.shape[1]
    slabs, ranks = lax.axis_size("slab"), lax.axis_size("rcv")
    chips = ranks // 2
    halo = 2 * steps
    share = size_y // slabs
    tile = size_y // ranks
    half = planes // 2
    window = share + 2 * halo
    wide = 2 * tile + 2 * halo
    total = planes * slabs
    rank = lax.axis_index("rcv")
    core, chip = rank % 2, rank // 2
    now, old, store = adjoint_now[0], adjoint_before[0], snapshot_store[0]

    cut = 2 * half * size_y
    own, sent, whole, *blocks = call(
        functools.partial(pack_body, (slabs, planes, size_y, size_z, share, halo, steps)),
        [(2, half, size_y, size_z), (cut + 8, size_z), (4 * planes, window, size_z)]
        + [(2 * half + 2 * planes, window, size_z)] * (slabs - 1),
        [now, old, courant_field, log_buoyancy],
        [receiver_cells, receiver_traces, residual_weights],
        [pltpu.VMEM((4, planes, size_y + 2 * halo, size_z), jnp.float32)],
    )
    got = swap(sent, "rcv", 1)
    blocks = [swap(block, "slab", d + 1) for d, block in enumerate(blocks)]
    others = [swap(block[: 2 * half], "rcv", 1) for block in blocks]

    flat = lambda a: a.reshape(-1, size_z)
    pair = own + got[:cut].reshape(2, half, size_y, size_z)
    pair = jnp.pad(pair, ((0, 0), (0, 0), (halo, halo), (0, 0)))
    info = sent[cut:] + got[cut:]
    received = []
    for d in range(chips):
        rows = lax.dynamic_slice_in_dim(pair, (chip ^ d) * 2 * tile, wide, 2)
        block = jnp.concatenate([flat(rows), info])
        received.append(swap(block, "rcv", 2 * d) if d else block)
    cut = 2 * half * wide
    summed = functools.reduce(jnp.add, [b[:cut] for b in received]).reshape(2 * half, wide, size_z)
    infos = jnp.concatenate([b[cut : cut + 2] for b in received])
    all_cells = infos[:, 0].astype(jnp.int32)
    all_traces = infos[:, 1 : 1 + steps]

    pick = functools.partial(lax.dynamic_index_in_dim, keepdims=False)
    tiles = store.reshape(planes, chips, 2, tile, size_z)
    tiles = jnp.stack([pick(tiles, core, 2), swap(pick(tiles, 1 - core, 2), "rcv", 1)])
    snaps = [pick(tiles, chip ^ d, 2) for d in range(chips)]
    snaps = [snaps[0]] + [swap(snaps[d], "rcv", 2 * d) for d in range(1, chips)]

    model = jnp.stack([courant_field, log_buoyancy])
    model = lax.dynamic_slice_in_dim(model, half * core, half, 1)
    model = jnp.pad(model, ((0, 0), (0, 0), (halo, halo), (0, 0)))
    model = lax.dynamic_slice_in_dim(model, chip * 2 * tile, wide, 2)
    block = jnp.concatenate([summed, model.reshape(2 * half, wide, size_z)])
    mine = [block] + [swap(block, "slab", d) for d in range(1, slabs)]

    def scratch(rows):
        rows = -(-rows // 16) * 16
        return (
            [pltpu.VMEM((total + 4, rows, size_z), jnp.float32)] * 4
            + [pltpu.VMEM((7, total, rows, size_z), jnp.float32)]
            + [pltpu.VMEM((2 * size_z, 2 * size_z), jnp.bfloat16), pltpu.VMEM((2 * rows, 2 * rows), jnp.bfloat16)]
        )

    finals = call(
        functools.partial(field_body, (slabs, planes, size_y, size_z, share, halo, steps)),
        [(planes, share, size_z)] * slabs,
        [whole] + blocks + others,
        [receiver_cells, receiver_traces],
        scratch(window),
        flops=40 * steps * total * window * size_z,
    )
    mine[1:] = lax.optimization_barrier(tuple(mine[1:]) + tuple(finals))[: slabs - 1]
    back = [finals[0]] + [swap(finals[d], "slab", d) for d in range(1, slabs)]
    theirs = [swap(b, "rcv", 1) for b in mine]
    (sensitivity,) = call(
        functools.partial(sum_body, (slabs, planes, size_y, size_z, tile, halo, steps, chips)),
        [(planes, tile, size_z)],
        mine + theirs + snaps,
        [owner_order, all_cells, all_traces],
        [pltpu.SMEM((4, 2 * chips + 1), jnp.int32), pltpu.VMEM((2 * chips, planes, tile, size_z), jnp.float32)]
        + scratch(sub_rows(tile, halo)),
        flops=40 * steps * total * sub_rows(tile, halo) * size_z,
    )
    (after,) = call(functools.partial(unpack_body, (slabs, share)), [(planes, size_y, size_z)], back, [], [])
    return (sensitivity, after[None])


def solution(mesh):
    placed = (
        P("rcv", "slab", None, None),
        P("rcv", "slab", None, None),
        P("slab", None, None),
        P("slab", None, None),
        P("rcv", "slab", None, None),
        P(),
        P("rcv"),
        P("rcv", None),
        P("rcv"),
    )

    return jax.shard_map(
        local,
        mesh=mesh,
        in_specs=placed,
        out_specs=(P("slab", "rcv", None), P("rcv", "slab", None, None)),
        check_vma=False,
    )
```

```python
import functools

import jax
import jax.numpy as jnp
from jax import lax
from jax.experimental import pallas as pl
from jax.experimental.pallas import tpu as pltpu
from jax.sharding import PartitionSpec as P


REACH = (1, -1, 2, -2)
GROUP = 8
SPARE = 4 << 20


VMEM = pl.BlockSpec(memory_space=pltpu.VMEM)
SMEM = pl.BlockSpec(memory_space=pltpu.SMEM)
HBM = pl.BlockSpec(memory_space=pltpu.HBM)


def swap(block, axis, mask):
    peers = lax.axis_size(axis)
    return lax.ppermute(block, axis, [(i, i ^ mask) for i in range(peers)])


def count(shape):
    return functools.reduce(lambda a, b: a * b, shape)


def call(body, outs, inputs, scalars, scratch, flops=0, far=()):
    size = 4 * (sum(x.size for x in (*inputs, *far)) + sum(count(o) for o in outs))
    held = sum(count(s.shape) * 4 for s in scratch if hasattr(s, "shape"))
    launch = pl.pallas_call(
        body,
        out_shape=[jax.ShapeDtypeStruct(o, jnp.float32) for o in outs],
        in_specs=[SMEM] * len(scalars) + [HBM] * len(far) + [VMEM] * len(inputs),
        out_specs=[VMEM] * len(outs),
        scratch_shapes=scratch,
        cost_estimate=pl.CostEstimate(flops=flops, bytes_accessed=size, transcendentals=0),
        compiler_params=pltpu.CompilerParams(vmem_limit_bytes=size + held + SPARE),
    )
    far = [pltpu.with_memory_space_constraint(x, pltpu.HBM) for x in far]
    return launch(*scalars, *far, *inputs)


def plan_rows(size_y, slabs, halo):
    inner = size_y - 2 * halo
    if inner > 0 and inner % (8 * slabs) == 0:
        stride = inner // slabs
        return stride, 0, stride + 2 * halo, stride + halo
    share = size_y // slabs
    return share, -halo, share + 2 * halo, share


def masks(chips):
    return [2**bit for bit in reversed(range(chips.bit_length() - 1))]


def position():
    rank = lax.axis_index("rcv")
    return lax.axis_index("slab"), rank % 2, rank // 2


def band(gap, near, far, centre):
    apart = jnp.abs(gap)
    weight = jnp.where(apart == 1, near, jnp.where(apart == 2, far, 0.0))
    if centre is None:
        return jnp.where(gap < 0, -weight, weight)
    return jnp.where(apart == 0, centre, weight)


def fill_bands(lanes, rows):
    size = lanes.shape[0] // 2
    gap = lax.broadcasted_iota(jnp.int32, lanes.shape, 0) % size - lax.broadcasted_iota(jnp.int32, lanes.shape, 1) % size
    column = lax.broadcasted_iota(jnp.int32, lanes.shape, 1)
    lanes[...] = jnp.where(column < size, band(gap, 16.0, -1.0, -90.0), band(gap, 8.0, -1.0, None)).astype(jnp.bfloat16)
    size = rows.shape[0] // 2
    gap = lax.broadcasted_iota(jnp.int32, rows.shape, 1) % size - lax.broadcasted_iota(jnp.int32, rows.shape, 0) % size
    row = lax.broadcasted_iota(jnp.int32, rows.shape, 0)
    rows[...] = jnp.where(row < size, band(gap, 16.0, -1.0, 0.0), band(gap, 8.0, -1.0, None)).astype(jnp.bfloat16)


def differences(ref, x, group, bands):
    lanes, rows = bands
    _, size_z = ref.shape[1:]
    parts = []
    for j in range(group):
        field = ref[x + j]
        high = field.astype(jnp.bfloat16)
        low = (field - high.astype(jnp.float32)).astype(jnp.bfloat16)
        parts.append((high, low))
    flat = jnp.concatenate([jnp.concatenate(p, axis=1) for p in parts], axis=0)
    along_z = jnp.dot(flat, lanes[...], preferred_element_type=jnp.float32)
    along_y = []
    for j in range(0, group, 2):
        pair = jnp.concatenate([jnp.concatenate(p, axis=0) for p in parts[j : j + 2]], axis=1)
        both = jnp.dot(rows[...], pair, preferred_element_type=jnp.float32)
        along_y += [both[:, i * size_z : (i + 1) * size_z] for i in range(2)]
    return along_z, along_y


def prepare(c_ref, b_ref, coef, bands, planes):
    count, size_z = b_ref.shape[1:]
    group = min(GROUP, planes)

    def some(g, carry):
        x = g * group
        along_z, along_y = differences(b_ref, x + 2, group, bands)
        for start in range(0, count, 8):
            rows = slice(start, start + 8)
            stack = [b_ref[x + k, rows, :] for k in range(group + 4)]
            for j in range(group):
                c = c_ref[x + j + 2, rows, :]
                scaled = (1.0 / 144.0) * c
                twelfth = (1.0 / 12.0) * c
                near = 16.0 * twelfth
                p1, m1, p2, m2 = [stack[j + 2 + k] for k in REACH]
                slope = scaled * (8.0 * (p1 - m1) - (p2 - m2))
                steep = 8.0 * slope
                weights = [near + steep, near - steep, -twelfth - slope, slope - twelfth, twelfth]
                weights.append(scaled * along_y[j][count + start : count + start + 8, :])
                weights.append(scaled * along_z[count * j + start : count * j + start + 8, size_z:])
                for i, weight in enumerate(weights):
                    coef[i, x + j, rows, :] = weight
        return carry

    lax.fori_loop(0, planes // group, some, 0)


def advance_planes(cur, old, coef, bands, row_lo, row_hi, x, group):
    count, size_z = cur.shape[1:]
    along_z, along_y = differences(cur, x + 2, group, bands)
    for start in range(row_lo, row_hi, 8):
        rows = slice(start, start + 8)
        stack = [cur[x + k, rows, :] for k in range(group + 4)]
        for j in range(group):
            terms = [coef[i, x + j, rows, :] * stack[j + 2 + k] for i, k in enumerate(REACH)]
            block = along_z[count * j + start : count * j + start + 8, :]
            curved, sloped = along_y[j][rows, :], along_y[j][count + start : count + start + 8, :]
            even = coef[4, x + j, rows, :] * (block[:, :size_z] + curved)
            odd = coef[5, x + j, rows, :] * sloped + coef[6, x + j, rows, :] * block[:, size_z:]
            base = (stack[j + 2] + stack[j + 2]) - old[x + j + 2, rows, :]
            old[x + j + 2, rows, :] = (base + (even + odd)) + ((terms[0] + terms[1]) + (terms[2] + terms[3]))


def advance(cur, old, coef, bands, row_lo, row_hi, total):
    group = min(GROUP, total)
    body = min(2 * group, total)

    def some(g, carry):
        for first in range(0, body, group):
            advance_planes(cur, old, coef, bands, row_lo, row_hi, g * body + first, group)
        return carry

    if body == total:
        some(0, 0)
    else:
        lax.fori_loop(0, total // body, some, 0)


def place(cell, first_row, size_y, size_z):
    return cell // (size_y * size_z), (cell // size_z) % size_y - first_row, cell % size_z


def inject(ref, spot, amplitude):
    x, row, z = spot
    size_z = ref.shape[2]
    base = pl.multiple_of((row // 8) * 8, 8)
    lane = lax.broadcasted_iota(jnp.int32, (8, size_z), 1)
    sub = lax.broadcasted_iota(jnp.int32, (8, size_z), 0)
    hit = (lane == z) & (sub == row - base)
    where = (x + 2, pl.ds(base, 8), slice(None))
    ref[where] = ref[where] + jnp.where(hit, amplitude, 0.0)


def clear_edges(refs, rows):
    for ref in refs:
        planes, count, size_z = ref.shape
        for x in (0, 1, planes - 2, planes - 1):
            ref[x, :, :] = jnp.zeros((count, size_z), jnp.float32)
        if rows < count:
            ref[:, rows:, :] = jnp.zeros((planes, count - rows, size_z), jnp.float32)


def span(step, rows):
    low, high = 2 * (step + 1), rows - 2 * (step + 1)
    return low // 8 * 8, min(rows, -(-high // 8) * 8)


def pack_body(dims, cells, weights, courant, logb, now, old, store, traces, *refs):
    slabs, planes, size_y, size_z, rows_of, tile, halo, steps = dims
    own, sent, kept, given, model, whole, *outs, wide, shot, trace, sems = refs
    stride, begin, window, _ = rows_of
    half = planes // 2
    slab, core, chip = position()
    weight = weights[0]
    inner = pl.ds(halo, size_y)
    copies = [
        pltpu.make_async_copy(ref, wide.at[i, :, inner, :], sems.at[i]) for i, ref in enumerate((courant, logb, now, old))
    ]
    copies += [pltpu.make_async_copy(store, shot, sems.at[4]), pltpu.make_async_copy(traces, trace, sems.at[5])]
    for i in (2, 3, 5, 4, 0, 1):
        copies[i].start()
    wide[:, :, 0:halo, :] = jnp.zeros((4, planes, halo, size_z), jnp.float32)
    wide[:, :, halo + size_y :, :] = jnp.zeros((4, planes, halo, size_z), jnp.float32)
    for i in (2, 3):
        copies[i].wait()
        for j in range(half):
            own[i - 2, j] = weight * wide[i, half * core + j, halo : halo + size_y, :]
            row = ((i - 2) * half + j) * size_y
            sent[row : row + size_y, :] = weight * wide[i, half * (1 - core) + j, halo : halo + size_y, :]
    copies[5].wait()
    ranks = size_y // tile
    lane = lax.broadcasted_iota(jnp.int32, (ranks, size_z), 1)
    sub = lax.broadcasted_iota(jnp.int32, (ranks, size_z), 0)
    row = jnp.where(lane == 0, cells[0].astype(jnp.float32), 0.0)
    for step in range(steps):
        row = jnp.where(lane == 1 + step, weight * trace[0, step], row)
    sent[2 * half * size_y :, :] = jnp.where(sub == 2 * chip + core, row, 0.0)
    copies[4].wait()
    for j in range(size_y // (2 * tile)):
        first, second = [shot[:, (2 * j + i) * tile : (2 * j + i + 1) * tile, :] for i in range(2)]
        kept[:, j] = jnp.where(core == 0, first, second)
        given[:, j] = jnp.where(core == 0, second, first)
    for i in (0, 1):
        copies[i].wait()
    for i in range(2):
        rows = pl.ds(pl.multiple_of(chip * 2 * tile, 8), 2 * tile + 2 * halo)
        model[i * half : (i + 1) * half] = wide[i, pl.ds(half * core, half), rows, :]
    for d in range(slabs):
        rows = pl.ds(pl.multiple_of((slab ^ d) * stride + begin + halo, 8), window)
        if d == 0:
            for i in range(4):
                whole[i * planes : (i + 1) * planes] = wide[i, :, rows, :]
            continue
        out = outs[d - 1]
        for i in range(2):
            out[i * half : (i + 1) * half] = wide[i, pl.ds(half * core, half), rows, :]
            out[2 * half + i * planes : 2 * half + (i + 1) * planes] = wide[2 + i, :, rows, :]


def halves(chip, mask):
    upper = (chip // mask) % 2
    return upper, 1 - upper


def pair_body(dims, own, sent, got, keep, send, wide):
    chips, half, size_y, tile, halo = dims
    rows = chips * tile + halo
    cut = 2 * half * size_y
    sides = halves(position()[2], chips // 2)
    for i in range(2 * half):
        wide[i] = own[i // half, i % half] + got[i * size_y : (i + 1) * size_y, :]
    for out, side in zip((keep, send), sides):
        taken = pl.ds(pl.multiple_of(side * (size_y - rows), 8), rows)
        for i in range(2 * half):
            out[i * rows : (i + 1) * rows, :] = wide[i, taken, :]
        out[2 * half * rows :, :] = sent[cut:, :] + got[cut:, :]


def halve_body(dims, held, got, keep, send, wide):
    chips, half, tile, halo, mask = dims
    whole = 4 * mask * tile + 2 * halo
    edge = 2 * mask == chips // 2
    before = whole - halo if edge else whole
    rows = 2 * mask * tile + 2 * halo
    chip = position()[2]
    offset = 0
    if edge:
        wide[...] = jnp.zeros(wide.shape, jnp.float32)
        offset = pl.multiple_of(halo * halves(chip, 2 * mask)[1], 8)
    for i in range(2 * half):
        part = slice(i * before, (i + 1) * before)
        wide[i, pl.ds(offset, before), :] = held[part, :] + got[part, :]
    for out, side in zip((keep, send), halves(chip, mask)):
        taken = pl.ds(pl.multiple_of(side * 2 * mask * tile, 8), rows)
        for i in range(2 * half):
            out[i * rows : (i + 1) * rows, :] = wide[i, taken, :]
        out[2 * half * rows :, :] = held[2 * half * before :, :] + got[2 * half * before :, :]


def shot_body(mask, held, got, keep, send):
    for out, side in zip((keep, send), halves(position()[2], mask)):
        taken = pl.ds(side * mask, mask)
        if len(held.shape) == 4:
            out[0], out[1] = held[:, taken], got[:, taken]
        else:
            out[: held.shape[0]], out[held.shape[0] :] = held[:, :, taken], got[:, :, taken]


def total_body(dims, model, held, got, out, infos):
    half, rows = dims
    for i in range(2 * half):
        taken = slice(i * rows, (i + 1) * rows)
        out[i] = held[taken, :] + got[taken, :]
    out[2 * half :] = model[...]
    infos[...] = held[2 * half * rows :, :] + got[2 * half * rows :, :]


def field_body(dims, cells, traces, whole, *refs):
    slabs, planes, size_y, size_z, rows_of, halo, steps = dims
    stride, begin, window, given = rows_of
    half = planes // 2
    total = planes * slabs
    blocks, others, outs = refs[: slabs - 1], refs[slabs - 1 : 2 * slabs - 2], refs[2 * slabs - 2 : 3 * slabs - 2]
    trace, sem, now, old, c_ref, b_ref, coef, *bands = refs[3 * slabs - 2 :]
    slab, core, _ = position()
    copy = pltpu.make_async_copy(traces, trace, sem.at[0])
    copy.start()
    clear_edges((now, old, c_ref, b_ref), window)
    fill_bands(*bands)
    inner = slice(0, window)
    for d in range(slabs):
        base = (slab ^ d) * planes + 2
        if d == 0:
            for i, ref in enumerate((c_ref, b_ref, now, old)):
                ref[pl.ds(base, planes), inner, :] = whole[i * planes : (i + 1) * planes]
            continue
        for i, ref in enumerate((now, old)):
            first = 2 * half + i * planes
            ref[pl.ds(base, planes), inner, :] = blocks[d - 1][first : first + planes]
        for i, ref in enumerate((c_ref, b_ref)):
            ref[pl.ds(base + half * core, half), inner, :] = blocks[d - 1][i * half : (i + 1) * half]
            ref[pl.ds(base + half * (1 - core), half), inner, :] = others[d - 1][i * half : (i + 1) * half]
    prepare(c_ref, b_ref, coef, bands, total)
    spot = place(cells[0], slab * stride + begin, size_y, size_z)
    copy.wait()
    for step in range(steps):
        low, high = span(step, window) if begin else (0, window)
        advance(now, old, coef, bands, low, high, total)

        @pl.when((spot[1] >= 0) & (spot[1] < window))
        def _(target=old, step=step):
            inject(target, spot, trace[0, step])

        now, old = old, now
    top = halo if begin else pl.multiple_of(jnp.where(slab == 0, 0, halo), 8)
    for d in range(slabs):
        outs[d][...] = now[pl.ds((slab ^ d) * planes + 2, planes), pl.ds(top, given), :]


def sub_rows(tile, halo):
    return 2 * halo + (tile if tile % 8 == 0 else 2 * tile)


def sum_body(dims, order, infos, *refs):
    slabs, planes, size_y, size_z, tile, halo, steps, groups = dims
    window = sub_rows(tile, halo)
    half = planes // 2
    total = planes * slabs
    mine, others, shots = refs[:slabs], refs[slabs : 2 * slabs], refs[2 * slabs : 2 * slabs + 2]
    out, spots, info, slots, sem, snaps, now, old, c_ref, b_ref, coef, *bands = refs[2 * slabs + 2 :]
    slab, core, chip = position()
    copies = [pltpu.make_async_copy(infos, info, sem.at[0]), pltpu.make_async_copy(order, slots, sem.at[1])]
    for copy in copies:
        copy.start()
    for d in range(2):
        snaps[d * groups : (d + 1) * groups] = shots[d][:, :, 0]
    clear_edges((now, old, c_ref, b_ref), window)
    fill_bands(*bands)
    inner = slice(0, window)
    offset = pl.multiple_of(core * tile, 8) if tile % 8 == 0 else 0
    taken = pl.ds(offset, window)
    for d in range(slabs):
        base = (slab ^ d) * planes + 2
        for i, ref in enumerate((now, old, c_ref, b_ref)):
            ref[pl.ds(base + half * core, half), inner, :] = mine[d][i * half : (i + 1) * half, taken, :]
            ref[pl.ds(base + half * (1 - core), half), inner, :] = others[d][i * half : (i + 1) * half, taken, :]
    prepare(c_ref, b_ref, coef, bands, total)
    first = chip * 2 * tile - halo + offset

    for copy in copies:
        copy.wait()

    def note(r, found):
        spot = place(info[r, 0].astype(jnp.int32), first, size_y, size_z)
        for i, value in enumerate(spot + (r,)):
            spots[i, found] = value
        return found + ((spot[1] >= 0) & (spot[1] < window)).astype(jnp.int32)

    inside = lax.fori_loop(0, 2 * groups, note, 0)
    acc = jnp.zeros((planes, tile, size_z), jnp.float32)
    for step in range(steps):
        low, high = span(step, window)
        if step == steps - 1:
            advance_planes(now, old, coef, bands, low, high, slab * planes, planes)
        else:
            advance(now, old, coef, bands, low, high, total)

        def add(i, carry, target=old, step=step):
            inject(target, (spots[0, i], spots[1, i], spots[2, i]), info[spots[3, i], 1 + step])
            return carry

        lax.fori_loop(0, inside, add, 0)
        now, old = old, now
        if step % 2 == 1:
            slot = slots[step // 2]
            away = (slot // 2) ^ chip
            piece = (slot % 2) ^ core
            for bit in range(groups.bit_length() - 1):
                piece = piece + ((away // 2**bit) % 2) * (groups // 2**bit)
            own = pl.ds(slab * planes + 2, planes)
            top = halo
            field = now[own, top : top + tile, :]
            if tile % 8:
                field = jnp.where(core == 0, field, now[own, top + tile : top + 2 * tile, :])
            acc = acc + field * snaps[piece]
    out[...] = acc


def unpack_body(dims, *refs):
    slabs, rows_of, halo = dims
    stride, begin, _, given = rows_of
    out = refs[slabs]
    slab, _, _ = position()
    for d in range(slabs):
        peer = slab ^ d
        if begin:
            out[:, pl.ds(pl.multiple_of(peer * stride, 8), given), :] = refs[d][...]
            continue
        top = pl.multiple_of(peer * stride + jnp.where(peer == 0, 0, halo), 8)
        out[:, pl.ds(top, stride), :] = refs[d][:, :stride, :]

        @pl.when((peer == 0) | (peer == slabs - 1))
        def _(top=top, piece=refs[d]):
            out[:, pl.ds(pl.multiple_of(top + stride, 8), halo), :] = piece[:, stride:, :]


def local(
    adjoint_now,
    adjoint_before,
    courant_field,
    log_buoyancy,
    snapshot_store,
    owner_order,
    receiver_cells,
    receiver_traces,
    residual_weights,
):
    planes, size_y, size_z = courant_field.shape
    steps = receiver_traces.shape[1]
    slabs, ranks = lax.axis_size("slab"), lax.axis_size("rcv")
    chips = ranks // 2
    halo = 2 * steps
    rows_of = plan_rows(size_y, slabs, halo)
    tile = size_y // ranks
    half = planes // 2
    _, _, window, returned = rows_of
    wide = 2 * tile + 2 * halo
    total = planes * slabs

    own, sent, kept, given, model, whole, *blocks = call(
        functools.partial(pack_body, (slabs, planes, size_y, size_z, rows_of, tile, halo, steps)),
        [(2, half, size_y, size_z), (2 * half * size_y + ranks, size_z)]
        + [(planes, chips, tile, size_z)] * 2
        + [(2 * half, wide, size_z), (4 * planes, window, size_z)]
        + [(2 * half + 2 * planes, window, size_z)] * (slabs - 1),
        [],
        [receiver_cells, residual_weights],
        [
            pltpu.VMEM((4, planes, size_y + 2 * halo, size_z), jnp.float32),
            pltpu.VMEM((planes, size_y, size_z), jnp.float32),
            pltpu.SMEM((1, steps), jnp.float32),
            pltpu.SemaphoreType.DMA((6,)),
        ],
        far=[courant_field, log_buoyancy, adjoint_now[0], adjoint_before[0], snapshot_store[0], receiver_traces],
    )
    got = swap(sent, "rcv", 1)
    blocks = [swap(block, "slab", d + 1) for d, block in enumerate(blocks)]
    others = [swap(block[: 2 * half], "rcv", 1) for block in blocks]

    depth = 2 * half
    rows = chips * tile + halo
    held, block = call(
        functools.partial(pair_body, (chips, half, size_y, tile, halo)),
        [(depth * rows + ranks, size_z)] * 2,
        [own, sent, got],
        [],
        [pltpu.VMEM((depth, size_y, size_z), jnp.float32)],
    )
    got = swap(block, "rcv", chips)
    for mask in masks(chips)[1:]:
        rows = 2 * mask * tile + 2 * halo
        held, block = call(
            functools.partial(halve_body, (chips, half, tile, halo, mask)),
            [(depth * rows + ranks, size_z)] * 2,
            [held, got],
            [],
            [pltpu.VMEM((depth, 4 * mask * tile + 2 * halo, size_z), jnp.float32)],
        )
        got = swap(block, "rcv", 2 * mask)
    block, infos = call(
        functools.partial(total_body, (half, wide)),
        [(4 * half, wide, size_z), (ranks, size_z)],
        [model, held, got],
        [],
        [],
    )
    mine = [block] + [swap(block, "slab", d) for d in range(1, slabs)]

    snaps = [kept, swap(given, "rcv", 1)]
    for mask in masks(chips):
        held, block = call(
            functools.partial(shot_body, mask), [(chips // mask, planes, mask, tile, size_z)] * 2, snaps, [], []
        )
        snaps = [held, swap(block, "rcv", 2 * mask)]

    def scratch(rows):
        rows = -(-rows // 16) * 16
        return (
            [pltpu.VMEM((total + 4, rows, size_z), jnp.float32)] * 4
            + [pltpu.VMEM((7, total, rows, size_z), jnp.float32)]
            + [pltpu.VMEM((2 * size_z, 2 * size_z), jnp.bfloat16), pltpu.VMEM((2 * rows, 2 * rows), jnp.bfloat16)]
        )

    finals = call(
        functools.partial(field_body, (slabs, planes, size_y, size_z, rows_of, halo, steps)),
        [(planes, returned, size_z)] * slabs,
        [whole] + blocks + others,
        [receiver_cells],
        [pltpu.SMEM((1, steps), jnp.float32), pltpu.SemaphoreType.DMA((1,))] + scratch(window),
        far=[receiver_traces],
        flops=40 * steps * total * window * size_z,
    )
    mine[1:] = lax.optimization_barrier(tuple(mine[1:]) + tuple(finals))[: slabs - 1]
    back = [finals[0]] + [swap(finals[d], "slab", d) for d in range(1, slabs)]
    theirs = [swap(b, "rcv", 1) for b in mine]
    (sensitivity,) = call(
        functools.partial(sum_body, (slabs, planes, size_y, size_z, tile, halo, steps, chips)),
        [(planes, tile, size_z)],
        [infos] + mine + theirs + snaps,
        [],
        [
            pltpu.SMEM((4, 2 * chips + 1), jnp.int32),
            pltpu.SMEM((2 * chips, size_z), jnp.float32),
            pltpu.SMEM(owner_order.shape, jnp.int32),
            pltpu.SemaphoreType.DMA((2,)),
            pltpu.VMEM((2 * chips, planes, tile, size_z), jnp.float32),
        ]
        + scratch(sub_rows(tile, halo)),
        far=[owner_order],
        flops=40 * steps * total * sub_rows(tile, halo) * size_z,
    )
    (after,) = call(functools.partial(unpack_body, (slabs, rows_of, halo)), [(planes, size_y, size_z)], back, [], [])
    return (sensitivity, after[None])


def solution(mesh):
    placed = (
        P("rcv", "slab", None, None),
        P("rcv", "slab", None, None),
        P("slab", None, None),
        P("slab", None, None),
        P("rcv", "slab", None, None),
        P(),
        P("rcv"),
        P("rcv", None),
        P("rcv"),
    )

    return jax.shard_map(
        local,
        mesh=mesh,
        in_specs=placed,
        out_specs=(P("slab", "rcv", None), P("rcv", "slab", None, None)),
        check_vma=False,
    )
```
